512 devices in a mesh: seq: 32 (over z, core), chan: 16 (over x, y).
Axes of the slice: x: 4, y: 4, z: 16, core: 2. Of those that a mesh axis runs over, the one named last changes fastest.
Arguments:
- hyena_in: bfloat16 [8192, 3, 4096], P('seq', None, 'chan'), may hold values from -6 to 6
- prior_kv: bfloat16 [127, 4096], P(None, 'chan'), may hold values from -6 to 6
- filters: float32 [256, 128], P('chan'), may hold values from -0.5 to 0.5
- gain: float32 [4096], replicated, may hold values from 0.5 to 1.5
- w_qkv: bfloat16 [4096, 3, 4096], P('seq', None, 'chan'), may hold values from -0.09375 to 0.09375
- cache_k: bfloat16 [4864, 4096], P('seq', 'chan'), may hold values from -110 to 110
- cache_v: bfloat16 [4864, 4096], P('seq', 'chan'), may hold values from -6 to 6
Outputs:
- attn_out: bfloat16 [8192, 4096], P('seq', 'chan')
The draws below stay inside these ranges and needn't reach their ends.
All inputs are finite; a program needn't handle non-finite values.
Results may differ from the reference program's by a relative error of at most 0.019.
The reference program's roundings to bfloat16 on the way (of `kv_prod`, `hyena_out`, `normed`, `qkv` and `probs`) count: a program that leaves them out, or rounds other values in their place, can miss the bound.
Values may be sent and summed in bfloat16 or wider, within the bound.
A program may use at most 128 MiB of HBM per device.

```python
import jax
import jax.numpy as jnp
from jax import lax

D = 4096
HEADS = 32
HEAD_DIM = 128
GROUP = 16
TAPS = 128
TOKENS = 8192
CACHE = 4864
FILTERS = 256
HIST = 127


def draw_cache_k(key, part):
    first_key = jax.random.fold_in(key, 0)
    values = jnp.clip(jax.random.normal(first_key, (CACHE, D), jnp.float32), -6.0, 6.0)
    return values.astype(jnp.bfloat16)


def level_of(own_key, extent, cuts, smallest, top_value):
    def one(dim, shards_of):
        steps = jax.random.uniform(jax.random.fold_in(jax.random.fold_in(own_key, 6), dim), (shards_of,), jnp.float32, smallest / len(cuts), top_value / len(cuts))
        return jnp.repeat(jnp.exp(steps), extent[dim] // shards_of).reshape((-1,) + (1,) * (len(extent) - dim - 1))

    factor_of = one(*cuts[0])
    for cut in cuts[1:]:
        factor_of = factor_of * one(*cut)
    return factor_of


def noise(rng, dims, scale, most, shards=(), kind=jnp.bfloat16):
    level = level_of(rng, dims, shards, -0.22, 0.18) if shards else 1.0
    array = jax.random.normal(rng, dims, jnp.float32) * scale * level
    return jnp.minimum(jnp.maximum(array, -most), most).astype(kind)


def setup_inputs(seed: int = 0) -> dict:
    seeds = jax.random.split(jax.random.key(seed), 8)
    return {
        "hyena_in": noise(seeds[0], (TOKENS, 3, D), 1.0, 6.0, ((0, 32), (2, 16))),
        "prior_kv": noise(seeds[1], (HIST, D), 1.0, 6.0, ((1, 16),)),
        "filters": noise(seeds[2], (FILTERS, TAPS), TAPS ** -0.5, 0.5, ((0, 16),), jnp.float32),
        "gain": jnp.clip(1.0 + 0.1 * jax.random.normal(seeds[3], (D,), jnp.float32), 0.5, 1.5),
        "w_qkv": noise(seeds[4], (D, 3, D), D ** -0.5, 0.09375, ((0, 32), (2, 16))),
        "cache_k": draw_cache_k(jax.random.fold_in(seeds[7], 71), 0),
        "cache_v": noise(seeds[6], (CACHE, D), 1.0, 6.0, ((0, 32), (1, 16))),
    }


def reference(hyena_in, prior_kv, filters, gain, w_qkv, cache_k, cache_v):
    stream_q = hyena_in[:, 0].astype(jnp.float32)
    kv_prod = (hyena_in[:, 1].astype(jnp.float32) * hyena_in[:, 2].astype(jnp.float32)).astype(jnp.bfloat16)
    extended = jnp.concatenate([prior_kv, kv_prod], axis=0).astype(jnp.float32)
    tap_table = jnp.repeat(filters, GROUP, axis=0).T

    def add_tap(tap_index, total):
        offset = (TAPS - 1 - tap_index).astype(jnp.int32)
        window = lax.dynamic_slice_in_dim(extended, offset, TOKENS, 0)
        coeff = lax.dynamic_index_in_dim(tap_table, tap_index.astype(jnp.int32), 0, keepdims=True)
        return total + coeff * window
    conv = lax.fori_loop(0, TAPS, add_tap, jnp.zeros((TOKENS, D), jnp.float32))
    hyena_out = (stream_q * conv).astype(jnp.bfloat16)
    as_float = hyena_out.astype(jnp.float32)
    mean_sq = lax.optimization_barrier(jnp.mean(as_float * as_float, axis=-1, keepdims=True))
    normed = (as_float * lax.rsqrt(mean_sq + 1e-06) * gain[None, :]).astype(jnp.bfloat16)
    qkv = jnp.dot(normed, w_qkv.reshape(D, 3 * D), preferred_element_type=jnp.float32).astype(jnp.bfloat16)
    qkv = qkv.reshape(TOKENS, 3, D)
    queries = jnp.moveaxis(qkv[:, 0].reshape(TOKENS, HEADS, HEAD_DIM), 1, 0)
    keys_all = jnp.concatenate([cache_k, qkv[:, 1]], axis=0).reshape(CACHE + TOKENS, HEADS, HEAD_DIM)
    vals_all = jnp.concatenate([cache_v, qkv[:, 2]], axis=0).reshape(CACHE + TOKENS, HEADS, HEAD_DIM)
    keys_all = jnp.moveaxis(keys_all, 1, 0)
    vals_all = jnp.moveaxis(vals_all, 1, 0)
    query_pos = jnp.arange(TOKENS, dtype=jnp.int32)
    key_pos = jnp.concatenate([jnp.full((CACHE,), -1, jnp.int32), jnp.arange(TOKENS, dtype=jnp.int32)])
    visible = key_pos[None, :] <= query_pos[:, None]
    scale = 1.0 / HEAD_DIM ** 0.5

    def one_head(operands):
        head_q, head_k, head_v = operands
        scores = jnp.dot(head_q, head_k.T, preferred_element_type=jnp.float32) * scale
        scores = jnp.where(visible, scores, jnp.float32(-1e+30))
        top = lax.optimization_barrier(jnp.max(scores, axis=-1, keepdims=True))
        weights = jnp.where(visible, jnp.exp(scores - top), jnp.float32(0.0))
        probs = weights.astype(jnp.bfloat16)
        summed = jnp.dot(probs, head_v, preferred_element_type=jnp.float32)
        return summed / lax.optimization_barrier(jnp.sum(weights, axis=-1, keepdims=True))
    result = lax.map(one_head, (queries, keys_all, vals_all))
    return jnp.moveaxis(result, 0, 1).reshape(TOKENS, D).astype(jnp.bfloat16)
```

```python
import jax
import jax.numpy as jnp
from jax import lax
from jax.experimental import pallas as pl
from jax.experimental.pallas import tpu as pltpu
from jax.sharding import PartitionSpec as P

MESH = pl.DeviceIdType.MESH
F32 = jnp.float32
BF16 = jnp.bfloat16
NZ = 16
NX = 4
NY = 4
ROWS = 256
WID = 256
HD = 128
TAPS = 128
D = NX * NY * WID
EPS = 1e-6


def place():
    s = lax.axis_index("seq")
    i = lax.axis_index("chan")
    return s // 2, lax.rem(s, 2), i // NY, lax.rem(i, NY)


def dev(z, c, x, y):
    return (lax.rem(z + NZ, NZ) * 2 + c, lax.rem(x + NX, NX) * NY + lax.rem(y + NY, NY))


def front_kernel(
    hy_ref, prior_ref, filt_ref, gain_ref, w_ref, qkv_ref,
    wsend, wbuf, kvp, halo, ext, shifts, table, hbuf, acc, ssq,
    sib_s, sib_r, halo_s, halo_r, up_s, up_r, dn_s, dn_r,
    a1_s, a1_r, b1_s, b1_r, a2_s, a2_r, b2_s, b2_r, hs_s, hs_r,
):
    z, c, x, y = place()
    me_i = x * NY + y
    sib = dev(z, 1 - c, x, y)
    above = dev(z + 1, c, x, y)
    below = dev(z - 1, c, x, y)
    nxt = dev(z + c, 1 - c, x, y)
    other = dev(z + 2 * c - 1, 1 - c, x, y)

    def remote(src, dst, ss, rs, to):
        return pltpu.make_async_remote_copy(
            src_ref=src, dst_ref=dst, send_sem=ss, recv_sem=rs, device_id=to, device_id_type=MESH
        )

    barrier = pltpu.get_barrier_semaphore()
    partners = [sib, above, below, other]
    partners += [dev(z, c, x + d, y) for d in (1, 2, 3)]
    partners += [dev(z, c, x, y + d) for d in (1, 2, 3)]
    for to in partners:
        pl.semaphore_signal(barrier, inc=1, device_id=to, device_id_type=MESH)

    mine = pl.ds(pl.multiple_of(c * HD, HD), HD)
    theirs = pl.ds(pl.multiple_of((1 - c) * HD, HD), HD)
    for j in range(3):
        wbuf[z, mine, j * HD : (j + 1) * HD] = w_ref[j, :, mine]
        wsend[:, j * HD : (j + 1) * HD] = w_ref[j, :, theirs]
    kvp[...] = (hy_ref[1].astype(F32) * hy_ref[2].astype(F32)).astype(BF16)
    pl.semaphore_wait(barrier, len(partners))

    wsib = remote(wsend, wbuf.at[z, mine, :], sib_s, sib_r, sib)
    wsib.start()
    hcopy = remote(kvp.at[pl.ds(ROWS - TAPS, TAPS)], halo, halo_s, halo_r, nxt)
    hcopy.start()

    def ring(k):
        src_up = lax.rem(z - (k - 1) + NZ, NZ)
        src_dn = lax.rem(z + (k - 1), NZ)
        if k < NZ // 2:
            su, sd = wbuf.at[src_up], wbuf.at[src_dn]
        else:
            su = wbuf.at[src_up, pl.ds(0, WID // 2)]
            sd = wbuf.at[src_dn, pl.ds(WID // 2, WID // 2)]
        return (
            remote(su, su, up_s.at[k - 1], up_r.at[k - 1], above),
            remote(sd, sd, dn_s.at[k - 1], dn_r.at[k - 1], below),
        )

    rings = [ring(k) for k in range(1, NZ // 2 + 1)]

    def ring_start(k):
        for cp in rings[k - 1]:
            cp.start()

    def ring_next(k):
        for cp in rings[k - 1]:
            cp.wait_recv()
        if k < NZ // 2:
            ring_start(k + 1)

    rev = (
        lax.broadcasted_iota(jnp.int32, (136, TAPS), 0)
        + lax.broadcasted_iota(jnp.int32, (136, TAPS), 1)
        == TAPS
    ).astype(F32)
    groups = filt_ref.shape[0]
    spread = (
        lax.broadcasted_iota(jnp.int32, (groups, WID), 0)
        == lax.broadcasted_iota(jnp.int32, (groups, WID), 1) // (WID // groups)
    ).astype(F32)
    reversed_taps = lax.dot_general(
        rev, filt_ref[...], (((1,), (1,)), ((), ())),
        precision=lax.Precision.HIGHEST, preferred_element_type=F32,
    )
    table[...] = lax.dot_general(
        reversed_taps, spread, (((1,), (0,)), ((), ())),
        precision=lax.Precision.HIGHEST, preferred_element_type=F32,
    )

    wsib.wait_recv()
    ring_start(1)
    hcopy.wait_recv()

    ext[pl.ds(0, TAPS), :] = halo[...].astype(F32)

    @pl.when(jnp.logical_and(z == 0, c == 0))
    def _():
        ext[pl.ds(1, TAPS - 1), :] = prior_ref[...].astype(F32)

    ext[pl.ds(TAPS, ROWS), :] = kvp[...].astype(F32)
    ext[pl.ds(TAPS + ROWS, 8), :] = jnp.zeros((8, WID), F32)
    total = TAPS + ROWS
    for r in range(8):
        shifts[r] = ext[r : r + total, :]

    half = ROWS // 2

    def conv_part(rows, lanes):
        def step(a, tot):
            base = pl.multiple_of(a * 8, 8)
            coeffs = table[pl.ds(base, 8), lanes]
            for r in range(8):
                window = shifts[r, pl.ds(pl.multiple_of(base + rows, 8), half), lanes]
                tot = tot + coeffs[r : r + 1] * window
            return tot

        conv = lax.fori_loop(0, TAPS // 8 + 1, step, jnp.zeros((half, HD), F32))
        out = (hy_ref[0, rows : rows + half, lanes].astype(F32) * conv).astype(BF16)
        hbuf[c, me_i, rows : rows + half, lanes] = out

    conv_part(0, slice(0, HD))
    conv_part(0, slice(HD, WID))
    ring_next(1)
    conv_part(half, slice(0, HD))
    conv_part(half, slice(HD, WID))

    first, second = pl.ds(0, half), pl.ds(half, half)

    def slot(ex, ey):
        return lax.rem(x - ex + NX, NX) * NY + lax.rem(y - ey + NY, NY)

    def piece(ex, ey, rows):
        return hbuf.at[c, slot(ex, ey), rows]

    def send_piece(ex, ey, rows, ss, rs, to):
        ref = piece(ex, ey, rows)
        return remote(ref, ref, ss, rs, to)

    order = (1, 3, 2)
    a1 = {d: send_piece(0, 0, first, a1_s.at[d], a1_r.at[d], dev(z, c, x + d, y)) for d in order}
    b1 = {d: send_piece(0, 0, second, b1_s.at[d], b1_r.at[d], dev(z, c, x, y + d)) for d in order}

    def landed(ex, ey, rows, ss, rs):
        ref = piece(ex, ey, rows)
        return remote(ref, ref, ss, rs, sib)

    a2 = {
        (e, d): send_piece(e, 0, first, a2_s.at[e, d], a2_r.at[e, d], dev(z, c, x, y + d))
        for e in range(4) for d in order
    }
    b2 = {
        (e, d): send_piece(0, e, second, b2_s.at[e, d], b2_r.at[e, d], dev(z, c, x + d, y))
        for e in range(4) for d in order
    }

    def to_sib(ex, ey):
        ref = hbuf.at[c, slot(ex, ey)]
        return remote(ref, ref, hs_s.at[ex, ey], hs_r.at[ex, ey], sib)

    own_sib = {(ex, ey): to_sib(ex, ey) for ex in range(4) for ey in range(4)}

    for d in order:
        a1[d].start()
        b1[d].start()
    for d in order:
        a2[0, d].start()
        b2[0, d].start()
    own_sib[0, 0].start()
    ring_next(2)
    for e in order:
        a1[e].wait_recv()
        for d in order:
            a2[e, d].start()
        b1[e].wait_recv()
        for d in order:
            b2[e, d].start()
    ring_next(3)
    for e in order:
        a2[0, e].wait_recv()
        own_sib[0, e].start()
        b2[0, e].wait_recv()
        own_sib[e, 0].start()
    ring_next(4)
    for n, (ex, ey) in enumerate([(ex, ey) for ex in order for ey in order]):
        a2[ex, ey].wait_recv()
        b2[ey, ex].wait_recv()
        own_sib[ex, ey].start()
        if n == 4:
            ring_next(5)
    ring_next(6)
    for key in own_sib:
        own_sib[key].wait_recv()

    ssq[...] = jnp.zeros_like(ssq)

    @pl.loop(0, NX * NY)
    def _(i):
        for h in range(2):
            blk = hbuf[h, i].astype(F32)
            sq = blk * blk
            ssq[pl.ds(h * ROWS, ROWS), :] += sq[:, :HD] + sq[:, HD:]

    inv = lax.rsqrt(jnp.sum(ssq[...], axis=1, keepdims=True) * (1.0 / D) + EPS)
    ssq[...] = jnp.broadcast_to(inv, ssq.shape)
    ring_next(7)
    ring_next(8)

    acc[...] = jnp.zeros_like(acc)

    @pl.loop(0, NX * NY)
    def _(i):
        g = gain_ref[pl.ds(i, 1), :]
        for h in range(2):
            rows = pl.ds(h * ROWS, ROWS)
            scale = ssq[rows, :]
            scale = jnp.concatenate([scale, scale], axis=1)
            normed = (hbuf[h, i].astype(F32) * scale * g).astype(BF16)
            acc[rows, :] += jnp.dot(normed, wbuf[i], preferred_element_type=F32)

    for j in range(3):
        qkv_ref[j] = acc[:, j * HD : (j + 1) * HD].astype(BF16)

    wsib.wait_send()
    hcopy.wait_send()
    for up, dn in rings:
        up.wait_send()
        dn.wait_send()
    for d in order:
        a1[d].wait_send()
        b1[d].wait_send()
    for key in a2:
        a2[key].wait_send()
        b2[key].wait_send()
    for key in own_sib:
        own_sib[key].wait_send()


def front(hyena_in, prior_kv, filters, gain, w_qkv):
    hy = jnp.transpose(hyena_in, (1, 0, 2))
    w = jnp.transpose(w_qkv, (1, 0, 2))
    g = gain.reshape(NX * NY, WID)
    dma = pltpu.SemaphoreType.DMA
    return pl.pallas_call(
        front_kernel,
        name="front",
        out_shape=jax.ShapeDtypeStruct((3, 2 * ROWS, HD), BF16),
        in_specs=[pl.BlockSpec(memory_space=pltpu.VMEM)] * 5,
        out_specs=pl.BlockSpec(memory_space=pltpu.VMEM),
        scratch_shapes=[
            pltpu.VMEM((HD, 3 * HD), BF16),
            pltpu.VMEM((NZ, WID, 3 * HD), BF16),
            pltpu.VMEM((ROWS, WID), BF16),
            pltpu.VMEM((TAPS, WID), BF16),
            pltpu.VMEM((TAPS + ROWS + 8, WID), F32),
            pltpu.VMEM((8, TAPS + ROWS, WID), F32),
            pltpu.VMEM((136, WID), F32),
            pltpu.VMEM((2, NX * NY, ROWS, WID), BF16),
            pltpu.VMEM((2 * ROWS, 3 * HD), F32),
            pltpu.VMEM((2 * ROWS, HD), F32),
            dma, dma, dma, dma,
            dma((8,)), dma((8,)), dma((8,)), dma((8,)),
            dma((4,)), dma((4,)), dma((4,)), dma((4,)),
            dma((4, 4)), dma((4, 4)), dma((4, 4)), dma((4, 4)),
            dma((4, 4)), dma((4, 4)),
        ],
        compiler_params=pltpu.CompilerParams(
            collective_id=1, has_side_effects=True, vmem_limit_bytes=40 * 1024 * 1024
        ),
    )(hy, prior_kv, filters, g, w)


def attend(qkv, cache_k, cache_v):
    rows_dev, heads_dev, head_size = ROWS, 2, HD
    cache_rows = cache_k.shape[0]
    stride = cache_rows + rows_dev
    my_index = lax.axis_index("seq")
    scale = 1.0 / head_size**0.5
    keys_local = jnp.concatenate([cache_k, qkv[:, 1]], axis=0)
    vals_local = jnp.concatenate([cache_v, qkv[:, 2]], axis=0)
    head_q = qkv[:, 0].reshape(rows_dev, heads_dev, head_size)
    query_pos = my_index * rows_dev + jnp.arange(rows_dev, dtype=jnp.int32)
    key_piece = lax.all_gather(keys_local, "seq", axis=0, tiled=True)
    val_piece = lax.all_gather(vals_local, "seq", axis=0, tiled=True)
    count = key_piece.shape[0]
    row_ids = jnp.arange(count, dtype=jnp.int32)
    source = row_ids // stride
    within = row_ids % stride
    key_pos = jnp.where(within < cache_rows, -1, source * rows_dev + within - cache_rows)
    visible = (key_pos[None, :] <= query_pos[:, None])[None]
    scores = (
        jnp.einsum(
            "qhd,khd->hqk", head_q, key_piece.reshape(count, heads_dev, head_size),
            preferred_element_type=F32,
        )
        * scale
    )
    scores = jnp.where(visible, scores, jnp.float32(-1e30))
    new_max = jnp.max(scores, axis=-1)
    weights = jnp.where(visible, jnp.exp(scores - new_max[..., None]), jnp.float32(0.0))
    new_sum = jnp.sum(weights, axis=-1)
    added = jnp.einsum(
        "hqk,khd->hqd", weights.astype(BF16), val_piece.reshape(count, heads_dev, head_size),
        preferred_element_type=F32,
    )
    result = jnp.transpose(added / new_sum[..., None], (1, 0, 2))
    return result.reshape(rows_dev, WID).astype(BF16)


def body(hyena_in, prior_kv, filters, gain, w_qkv, cache_k, cache_v):
    qkv = front(hyena_in, prior_kv, filters, gain, w_qkv)
    c = lax.rem(lax.axis_index("seq"), 2)
    own = lax.dynamic_slice_in_dim(qkv, c * ROWS, ROWS, 1)
    away = lax.dynamic_slice_in_dim(qkv, (1 - c) * ROWS, ROWS, 1)
    pairs = [(2 * z + k, 2 * z + 1 - k) for z in range(NZ) for k in range(2)]
    came = lax.ppermute(away, "seq", pairs)
    both = jnp.concatenate([jnp.where(c == 0, own, came), jnp.where(c == 0, came, own)], axis=2)
    return attend(jnp.transpose(both, (1, 0, 2)), cache_k, cache_v)


def solution(mesh):
    return jax.shard_map(
        body,
        mesh=mesh,
        in_specs=(
            P("seq", None, "chan"),
            P(None, "chan"),
            P("chan", None),
            P(),
            P("seq", None, "chan"),
            P("seq", "chan"),
            P("seq", "chan"),
        ),
        out_specs=P("seq", "chan"),
        check_vma=False,
    )
```

```python
import jax
import jax.numpy as jnp
from jax import lax
from jax.experimental import pallas as pl
from jax.experimental.pallas import tpu as pltpu
from jax.sharding import PartitionSpec as P

MESH = pl.DeviceIdType.MESH
F32 = jnp.float32
BF16 = jnp.bfloat16
NZ = 16
NX = 4
NY = 4
ROWS = 256
WID = 256
HD = 128
TAPS = 128
D = NX * NY * WID
EPS = 1e-6
SCALE = 1.4426950408889634 / HD**0.5


def place():
    s = lax.axis_index("seq")
    i = lax.axis_index("chan")
    return s // 2, lax.rem(s, 2), i // NY, lax.rem(i, NY)


def dev(z, c, x, y):
    return (lax.rem(z + NZ, NZ) * 2 + c, lax.rem(x + NX, NX) * NY + lax.rem(y + NY, NY))


def whole_kernel(
    hy_ref, prior_ref, filt_ref, gain_ref, w_ref, ck_ref, cv_ref, out_ref,
    wsend, wbuf, kvp, halo, ext, shifts, table, hbuf, acc, ssq,
    sib_s, sib_r, halo_s, halo_r, up_s, up_r, dn_s, dn_r,
    a1_s, a1_r, b1_s, b1_r, a2_s, a2_r, b2_s, b2_r, hs_s, hs_r,
    csib, kold, vold, knew, vnew, qbuf, po, pm, ps, osend, oin, tsend, tin, oswap,
    cs_s, cs_r, q_s, q_r, o_s, o_r, t_s, t_r, x_s, x_r,
):
    z, c, x, y = place()
    me_i = x * NY + y
    sib = dev(z, 1 - c, x, y)
    above = dev(z + 1, c, x, y)
    below = dev(z - 1, c, x, y)
    nxt = dev(z + c, 1 - c, x, y)
    other = dev(z + 2 * c - 1, 1 - c, x, y)

    def remote(src, dst, ss, rs, to):
        return pltpu.make_async_remote_copy(
            src_ref=src, dst_ref=dst, send_sem=ss, recv_sem=rs, device_id=to, device_id_type=MESH
        )

    barrier = pltpu.get_barrier_semaphore()
    partners = [sib, above, below, other]
    partners += [dev(z, c, x + d, y) for d in (1, 2, 3)]
    partners += [dev(z, c, x, y + d) for d in (1, 2, 3)]
    for to in partners:
        pl.semaphore_signal(barrier, inc=1, device_id=to, device_id_type=MESH)

    mine = pl.ds(pl.multiple_of(c * HD, HD), HD)
    theirs = pl.ds(pl.multiple_of((1 - c) * HD, HD), HD)
    for j in range(3):
        wbuf[z, mine, j * HD : (j + 1) * HD] = w_ref[j, :, mine]
        wsend[:, j * HD : (j + 1) * HD] = w_ref[j, :, theirs]
    kvp[...] = (hy_ref[1].astype(F32) * hy_ref[2].astype(F32)).astype(BF16)
    pl.semaphore_wait(barrier, len(partners))

    wsib = remote(wsend, wbuf.at[z, mine, :], sib_s, sib_r, sib)
    wsib.start()
    csibs = [
        remote(ref.at[:, theirs], csib.at[n], cs_s.at[n], cs_r.at[n], sib)
        for n, ref in enumerate((ck_ref, cv_ref))
    ]
    for cp in csibs:
        cp.start()
    hcopy = remote(kvp.at[pl.ds(ROWS - TAPS, TAPS)], halo, halo_s, halo_r, nxt)
    hcopy.start()

    def ring(k):
        src_up = lax.rem(z - (k - 1) + NZ, NZ)
        src_dn = lax.rem(z + (k - 1), NZ)
        if k < NZ // 2:
            su, sd = wbuf.at[src_up], wbuf.at[src_dn]
        else:
            su = wbuf.at[src_up, pl.ds(0, WID // 2)]
            sd = wbuf.at[src_dn, pl.ds(WID // 2, WID // 2)]
        return (
            remote(su, su, up_s.at[k - 1], up_r.at[k - 1], above),
            remote(sd, sd, dn_s.at[k - 1], dn_r.at[k - 1], below),
        )

    rings = [ring(k) for k in range(1, NZ // 2 + 1)]

    def ring_start(k):
        for cp in rings[k - 1]:
            cp.start()

    def ring_next(k):
        for cp in rings[k - 1]:
            cp.wait_recv()
        if k < NZ // 2:
            ring_start(k + 1)

    rev = (
        lax.broadcasted_iota(jnp.int32, (136, TAPS), 0)
        + lax.broadcasted_iota(jnp.int32, (136, TAPS), 1)
        == TAPS
    ).astype(F32)
    groups = filt_ref.shape[0]
    spread = (
        lax.broadcasted_iota(jnp.int32, (groups, WID), 0)
        == lax.broadcasted_iota(jnp.int32, (groups, WID), 1) // (WID // groups)
    ).astype(F32)
    reversed_taps = lax.dot_general(
        rev, filt_ref[...], (((1,), (1,)), ((), ())),
        precision=lax.Precision.HIGHEST, preferred_element_type=F32,
    )
    table[...] = lax.dot_general(
        reversed_taps, spread, (((1,), (0,)), ((), ())),
        precision=lax.Precision.HIGHEST, preferred_element_type=F32,
    )

    wsib.wait_recv()
    ring_start(1)
    hcopy.wait_recv()

    ext[pl.ds(0, TAPS), :] = halo[...].astype(F32)

    @pl.when(jnp.logical_and(z == 0, c == 0))
    def _():
        ext[pl.ds(1, TAPS - 1), :] = prior_ref[...].astype(F32)

    ext[pl.ds(TAPS, ROWS), :] = kvp[...].astype(F32)
    ext[pl.ds(TAPS + ROWS, 8), :] = jnp.zeros((8, WID), F32)
    total = TAPS + ROWS
    for r in range(8):
        shifts[r] = ext[r : r + total, :]

    half = ROWS // 2

    def conv_part(rows, lanes):
        def step(a, tot):
            base = pl.multiple_of(a * 8, 8)
            coeffs = table[pl.ds(base, 8), lanes]
            for r in range(8):
                window = shifts[r, pl.ds(pl.multiple_of(base + rows, 8), half), lanes]
                tot = tot + coeffs[r : r + 1] * window
            return tot

        conv = lax.fori_loop(0, TAPS // 8 + 1, step, jnp.zeros((half, HD), F32))
        out = (hy_ref[0, rows : rows + half, lanes].astype(F32) * conv).astype(BF16)
        hbuf[c, me_i, rows : rows + half, lanes] = out

    conv_part(0, slice(0, HD))
    conv_part(0, slice(HD, WID))
    ring_next(1)
    conv_part(half, slice(0, HD))
    conv_part(half, slice(HD, WID))

    first, second = pl.ds(0, half), pl.ds(half, half)

    def slot(ex, ey):
        return lax.rem(x - ex + NX, NX) * NY + lax.rem(y - ey + NY, NY)

    def piece(ex, ey, rows):
        return hbuf.at[c, slot(ex, ey), rows]

    def send_piece(ex, ey, rows, ss, rs, to):
        ref = piece(ex, ey, rows)
        return remote(ref, ref, ss, rs, to)

    order = (1, 3, 2)
    a1 = {d: send_piece(0, 0, first, a1_s.at[d], a1_r.at[d], dev(z, c, x + d, y)) for d in order}
    b1 = {d: send_piece(0, 0, second, b1_s.at[d], b1_r.at[d], dev(z, c, x, y + d)) for d in order}

    def landed(ex, ey, rows, ss, rs):
        ref = piece(ex, ey, rows)
        return remote(ref, ref, ss, rs, sib)

    a2 = {
        (e, d): send_piece(e, 0, first, a2_s.at[e, d], a2_r.at[e, d], dev(z, c, x, y + d))
        for e in range(4) for d in order
    }
    b2 = {
        (e, d): send_piece(0, e, second, b2_s.at[e, d], b2_r.at[e, d], dev(z, c, x + d, y))
        for e in range(4) for d in order
    }

    def to_sib(ex, ey):
        ref = hbuf.at[c, slot(ex, ey)]
        return remote(ref, ref, hs_s.at[ex, ey], hs_r.at[ex, ey], sib)

    own_sib = {(ex, ey): to_sib(ex, ey) for ex in range(4) for ey in range(4)}

    for d in order:
        a1[d].start()
        b1[d].start()
    for d in order:
        a2[0, d].start()
        b2[0, d].start()
    own_sib[0, 0].start()
    ring_next(2)
    for e in order:
        a1[e].wait_recv()
        for d in order:
            a2[e, d].start()
        b1[e].wait_recv()
        for d in order:
            b2[e, d].start()
    ring_next(3)
    for e in order:
        a2[0, e].wait_recv()
        own_sib[0, e].start()
        b2[0, e].wait_recv()
        own_sib[e, 0].start()
    ring_next(4)
    for n, (ex, ey) in enumerate([(ex, ey) for ex in order for ey in order]):
        a2[ex, ey].wait_recv()
        b2[ey, ex].wait_recv()
        own_sib[ex, ey].start()
        if n == 4:
            ring_next(5)
    ring_next(6)
    for key in own_sib:
        own_sib[key].wait_recv()

    ssq[...] = jnp.zeros_like(ssq)

    @pl.loop(0, NX * NY)
    def _(i):
        for h in range(2):
            blk = hbuf[h, i].astype(F32)
            sq = blk * blk
            ssq[pl.ds(h * ROWS, ROWS), :] += sq[:, :HD] + sq[:, HD:]

    inv = lax.rsqrt(jnp.sum(ssq[...], axis=1, keepdims=True) * (1.0 / D) + EPS)
    ssq[...] = jnp.broadcast_to(inv, ssq.shape)
    ring_next(7)
    for n, (ref, buf) in enumerate(((ck_ref, kold), (cv_ref, vold))):
        csibs[n].wait_recv()
        both = [ref[:, mine].astype(F32), csib[n].astype(F32)]
        buf[...] = jnp.concatenate(both, axis=0).astype(BF16)
    ring_next(8)

    acc[...] = jnp.zeros_like(acc)

    @pl.loop(0, NX * NY)
    def _(i):
        g = gain_ref[pl.ds(i, 1), :]
        for h in range(2):
            rows = pl.ds(h * ROWS, ROWS)
            scale = ssq[rows, :]
            scale = jnp.concatenate([scale, scale], axis=1)
            normed = (hbuf[h, i].astype(F32) * scale * g).astype(BF16)
            acc[rows, :] += jnp.dot(normed, wbuf[i], preferred_element_type=F32)

    qbuf[z] = acc[:, :HD].astype(BF16)
    knew[...] = acc[:, HD : 2 * HD].astype(BF16)
    vnew[...] = acc[:, 2 * HD :].astype(BF16)

    def at(way, k, h):
        return (way * 8 + k - 1) * 2 + h

    def rows_of(h):
        return pl.ds(pl.multiple_of(h * ROWS, ROWS), ROWS)

    def source(way, k):
        return lax.rem(z + (2 * way - 1) * k + NZ, NZ)

    def along(way):
        return dev(z + 1 - 2 * way, c, x, y)

    def query(way, k, h):
        ref = qbuf.at[source(way, k - 1), rows_of(h)]
        n = at(way, k, h)
        return remote(ref, ref, q_s.at[n], q_r.at[n], along(way))

    def scores(q, keys):
        s = lax.dot_general(q, keys, (((1,), (1,)), ((), ())), preferred_element_type=F32)
        return s * SCALE

    def part(slot, pairs):
        m = pairs[0][0].max(axis=1, keepdims=True)
        for s, _ in pairs[1:]:
            m = jnp.maximum(m, s.max(axis=1, keepdims=True))
        o = l = None
        for s, vals in pairs:
            p = jnp.exp2(s - m)
            a = jnp.dot(p.astype(BF16), vals[...], preferred_element_type=F32)
            b = p.sum(axis=1, keepdims=True)
            o, l = (a, b) if o is None else (o + a, l + b)
        po[slot] = o
        pm[slot] = jnp.broadcast_to(m, (ROWS, HD))
        ps[slot] = jnp.broadcast_to(l, (ROWS, HD))

    def visit(way, k, h):
        slot = at(way, k, h)
        src = source(way, k)

        @pl.when(src > z)
        def _():
            q = qbuf[src, rows_of(h)]
            part(slot, [(scores(q, knew[...]), vnew), (scores(q, kold[...]), vold)])

        @pl.when(src < z)
        def _():
            q = qbuf[src, rows_of(h)]
            part(slot, [(scores(q, kold[...]), vold)])

    for h in range(2):
        for way in range(2):
            query(way, 1, h).start()

    @pl.loop(0, 2)
    def _(h):
        q = qbuf[z, rows_of(h)]
        s = scores(q, knew[...])
        t = h * ROWS + lax.broadcasted_iota(jnp.int32, s.shape, 0)
        s = jnp.where(lax.broadcasted_iota(jnp.int32, s.shape, 1) <= t, s, -1e30)
        part(32 + h, [(s, vnew), (scores(q, kold[...]), vold)])

    def merged(slot, msg):
        msg_m = jnp.transpose(jnp.broadcast_to(tin[msg, 0:1], (HD, ROWS)))
        msg_s = jnp.transpose(jnp.broadcast_to(tin[msg, 4:5], (HD, ROWS)))
        m = jnp.maximum(pm[slot], msg_m)
        mine_f = jnp.exp2(pm[slot] - m)
        msg_f = jnp.exp2(msg_m - m)
        o = po[slot] * mine_f + oin[msg].astype(F32) * msg_f
        return o, m, ps[slot] * mine_f + msg_s * msg_f

    def answer(way, k, h):
        n = at(way, k, h)
        dst = way * 16 + (k - 1) * 2 + h
        to = along(1 - way)
        return (
            remote(osend.at[n], oin.at[dst], o_s.at[n], o_r.at[dst], to),
            remote(tsend.at[n], tin.at[dst], t_s.at[n], t_r.at[dst], to),
        )

    def arrive(way, k, h):
        for cp in answer(way, k + 1, h):
            cp.wait_recv()

    def give(way, k, h, last):
        slot = at(way, k, h)
        if last:
            o, m, l = po[slot], pm[slot], ps[slot]
        else:
            arrive(way, k, h)
            o, m, l = merged(slot, way * 16 + k * 2 + h)
        osend[slot] = o.astype(BF16)
        lane = lax.broadcasted_iota(jnp.int32, (ROWS, HD), 1)
        tsend[slot] = jnp.transpose(jnp.where(lax.rem(lane, 8) < 4, m, l))[:8]
        for cp in answer(way, k, h):
            cp.start()

    @pl.loop(0, 24)
    def _(n):
        k, h, way = n // 4 + 1, lax.rem(n // 2, 2), lax.rem(n, 2)
        query(way, k, h).wait_recv()
        query(way, k + 1, h).start()
        visit(way, k, h)

    @pl.loop(0, 2)
    def _(way):
        query(way, 7, way).wait_recv()
        query(way, 8, way).start()
        visit(way, 7, way)

    @pl.loop(0, 2)
    def _(way):
        query(way, 7, 1 - way).wait_recv()
        visit(way, 7, 1 - way)
        give(way, 7, 1 - way, True)

    @pl.loop(0, 2)
    def _(way):
        query(way, 8, way).wait_recv()
        visit(way, 8, way)
        give(way, 8, way, True)

    @pl.loop(0, 26)
    def _(n):
        k = jnp.where(n < 2, 7, 6 - (n - 2) // 4)
        way = lax.rem(n, 2)
        h = jnp.where(n < 2, way, lax.rem((n + 2) // 2, 2))
        give(way, k, h, False)

    def finish(h):
        slot = 32 + h
        for way in range(2):
            arrive(way, 0, h)
            o, m, l = merged(slot, way * 16 + h)
            po[slot], pm[slot], ps[slot] = o, m, l
        return (o / l).astype(BF16)

    oswap[0] = finish(1 - c)
    swap = remote(oswap.at[0], oswap.at[1], x_s, x_r, sib)
    swap.start()
    out_ref[:, mine] = finish(c)
    swap.wait_recv()
    out_ref[:, theirs] = oswap[1]

    swap.wait_send()

    @pl.loop(0, 30)
    def _(n):
        k, h, way = n // 4 + 1, lax.rem(n // 2, 2), lax.rem(n, 2)
        h = jnp.where(n < 28, h, way)
        query(way, k, h).wait_send()
        for cp in answer(way, k, h):
            cp.wait_send()

    for cp in csibs:
        cp.wait_send()
    wsib.wait_send()
    hcopy.wait_send()
    for up, dn in rings:
        up.wait_send()
        dn.wait_send()
    for d in order:
        a1[d].wait_send()
        b1[d].wait_send()
    for key in a2:
        a2[key].wait_send()
        b2[key].wait_send()
    for key in own_sib:
        own_sib[key].wait_send()


def body(hyena_in, prior_kv, filters, gain, w_qkv, cache_k, cache_v):
    hy = jnp.transpose(hyena_in, (1, 0, 2))
    w = jnp.transpose(w_qkv, (1, 0, 2))
    g = gain.reshape(NX * NY, WID)
    old = cache_k.shape[0]
    dma = pltpu.SemaphoreType.DMA
    vmem = pltpu.VMEM
    return pl.pallas_call(
        whole_kernel,
        name="whole",
        out_shape=jax.ShapeDtypeStruct((ROWS, WID), BF16),
        in_specs=[pl.BlockSpec(memory_space=pltpu.VMEM)] * 7,
        out_specs=pl.BlockSpec(memory_space=pltpu.VMEM),
        scratch_shapes=[
            vmem((HD, 3 * HD), BF16),
            vmem((NZ, WID, 3 * HD), BF16),
            vmem((ROWS, WID), BF16),
            vmem((TAPS, WID), BF16),
            vmem((TAPS + ROWS + 8, WID), F32),
            vmem((8, TAPS + ROWS, WID), F32),
            vmem((136, WID), F32),
            vmem((2, NX * NY, ROWS, WID), BF16),
            vmem((2 * ROWS, 3 * HD), F32),
            vmem((2 * ROWS, HD), F32),
            dma, dma, dma, dma,
            dma((8,)), dma((8,)), dma((8,)), dma((8,)),
            dma((4,)), dma((4,)), dma((4,)), dma((4,)),
            dma((4, 4)), dma((4, 4)), dma((4, 4)), dma((4, 4)),
            dma((4, 4)), dma((4, 4)),
            vmem((2, old, HD), BF16),
            vmem((2 * old, HD), BF16),
            vmem((2 * old, HD), BF16),
            vmem((2 * ROWS, HD), BF16),
            vmem((2 * ROWS, HD), BF16),
            vmem((NZ, 2 * ROWS, HD), BF16),
            vmem((34, ROWS, HD), F32),
            vmem((34, ROWS, HD), F32),
            vmem((34, ROWS, HD), F32),
            vmem((32, ROWS, HD), BF16),
            vmem((32, ROWS, HD), BF16),
            vmem((32, 8, ROWS), F32),
            vmem((32, 8, ROWS), F32),
            vmem((2, ROWS, HD), BF16),
            dma((2,)), dma((2,)),
            dma((32,)), dma((32,)), dma((32,)), dma((32,)), dma((32,)), dma((32,)),
            dma, dma,
        ],
        compiler_params=pltpu.CompilerParams(
            collective_id=1, has_side_effects=True, vmem_limit_bytes=56 * 1024 * 1024
        ),
    )(hy, prior_kv, filters, g, w, cache_k, cache_v)


def solution(mesh):
    return jax.shard_map(
        body,
        mesh=mesh,
        in_specs=(
            P("seq", None, "chan"),
            P(None, "chan"),
            P("chan", None),
            P(),
            P("seq", None, "chan"),
            P("seq", "chan"),
            P("seq", "chan"),
        ),
        out_specs=P("seq", "chan"),
        check_vma=False,
    )
```

```python
import jax
import jax.numpy as jnp
from jax import lax
from jax.experimental import pallas as pl
from jax.experimental.pallas import tpu as pltpu
from jax.sharding import PartitionSpec as P

MESH = pl.DeviceIdType.MESH
F32 = jnp.float32
BF16 = jnp.bfloat16
NZ = 16
NX = 4
NY = 4
ROWS = 256
WID = 256
HD = 128
TAPS = 128
D = NX * NY * WID
EPS = 1e-6
SUB = 4
HB = 2 * ROWS // SUB
SCALE = 1.4426950408889634 / HD**0.5


def place():
    s = lax.axis_index("seq")
    i = lax.axis_index("chan")
    return s // 2, lax.rem(s, 2), i // NY, lax.rem(i, NY)


def dev(z, c, x, y):
    return (lax.rem(z + NZ, NZ) * 2 + c, lax.rem(x + NX, NX) * NY + lax.rem(y + NY, NY))


def whole_kernel(
    hy_ref, prior_ref, filt_ref, gain_ref, w_ref, ck_ref, cv_ref, out_ref,
    wsend, wbuf, kvp, halo, ext, shifts, table, hbuf, acc, ssq,
    sib_s, sib_r, halo_s, halo_r, up_s, up_r, dn_s, dn_r,
    a1_s, a1_r, b1_s, b1_r, a2_s, a2_r, b2_s, b2_r, hs_s, hs_r,
    csib, kold, vold, knew, vnew, qbuf, po, pm, ps, osend, oin, tsend, tin, oswap,
    cs_s, cs_r, q_s, q_r, o_s, o_r, t_s, t_r, x_s, x_r,
):
    z, c, x, y = place()
    me_i = x * NY + y
    sib = dev(z, 1 - c, x, y)
    above = dev(z + 1, c, x, y)
    below = dev(z - 1, c, x, y)
    nxt = dev(z + c, 1 - c, x, y)
    other = dev(z + 2 * c - 1, 1 - c, x, y)

    def remote(src, dst, ss, rs, to):
        return pltpu.make_async_remote_copy(
            src_ref=src, dst_ref=dst, send_sem=ss, recv_sem=rs, device_id=to, device_id_type=MESH
        )

    barrier = pltpu.get_barrier_semaphore()
    partners = [sib, above, below, other]
    partners += [dev(z, c, x + d, y) for d in (1, -1)]
    partners += [dev(z, c, x, y + d) for d in (1, -1)]
    for to in partners:
        pl.semaphore_signal(barrier, inc=1, device_id=to, device_id_type=MESH)

    mine = pl.ds(pl.multiple_of(c * HD, HD), HD)
    theirs = pl.ds(pl.multiple_of((1 - c) * HD, HD), HD)
    for j in range(3):
        wbuf[z, mine, j * HD : (j + 1) * HD] = w_ref[j, :, mine]
        wsend[:, j * HD : (j + 1) * HD] = w_ref[j, :, theirs]
    kvp[...] = (hy_ref[1].astype(F32) * hy_ref[2].astype(F32)).astype(BF16)
    pl.semaphore_wait(barrier, len(partners))

    wsib = remote(wsend, wbuf.at[z, mine, :], sib_s, sib_r, sib)
    wsib.start()
    csibs = [
        remote(ref.at[:, theirs], csib.at[n], cs_s.at[n], cs_r.at[n], sib)
        for n, ref in enumerate((ck_ref, cv_ref))
    ]
    for cp in csibs:
        cp.start()
    hcopy = remote(kvp.at[pl.ds(ROWS - TAPS, TAPS)], halo, halo_s, halo_r, nxt)
    hcopy.start()

    def goes(way, k, j):
        return k < NZ // 2 or (k == NZ // 2 and (j < SUB // 2) == (way == 0))

    def weight(way, k, j):
        src = lax.rem(z + (2 * way - 1) * (k - 1) + NZ, NZ)
        ref = wbuf.at[src, pl.ds(pl.multiple_of(j * (WID // SUB), WID // SUB), WID // SUB)]
        n = (k - 1) * SUB + j
        ss, rs = (up_s, up_r) if way == 0 else (dn_s, dn_r)
        return remote(ref, ref, ss.at[n], rs.at[n], (above, below)[way])

    def ring_next(n):
        k, j = n // SUB + 1, n % SUB
        for way in range(2):
            if goes(way, k, j):
                weight(way, k, j).wait_recv()
            if goes(way, k + 1, j):
                weight(way, k + 1, j).start()

    served = [0]

    def serve(count):
        begin, end = served[0], served[0] + count
        served[0] = end
        looped = min(end, SUB * (NZ // 2 - 2))
        if looped - begin > 1:

            @pl.loop(begin, looped)
            def _(n):
                k, j = n // SUB + 1, lax.rem(n, SUB)
                for way in range(2):
                    weight(way, k, j).wait_recv()
                    weight(way, k + 1, j).start()

            begin = looped
        for n in range(begin, end):
            ring_next(n)

    rev = (
        lax.broadcasted_iota(jnp.int32, (136, TAPS), 0)
        + lax.broadcasted_iota(jnp.int32, (136, TAPS), 1)
        == TAPS
    ).astype(F32)
    groups = filt_ref.shape[0]
    spread = (
        lax.broadcasted_iota(jnp.int32, (groups, WID), 0)
        == lax.broadcasted_iota(jnp.int32, (groups, WID), 1) // (WID // groups)
    ).astype(F32)
    reversed_taps = lax.dot_general(
        rev, filt_ref[...], (((1,), (1,)), ((), ())),
        precision=lax.Precision.HIGHEST, preferred_element_type=F32,
    )
    table[...] = lax.dot_general(
        reversed_taps, spread, (((1,), (0,)), ((), ())),
        precision=lax.Precision.HIGHEST, preferred_element_type=F32,
    )

    wsib.wait_recv()
    for j in range(SUB):
        for way in range(2):
            weight(way, 1, j).start()
    hcopy.wait_recv()

    ext[pl.ds(0, TAPS), :] = halo[...].astype(F32)

    @pl.when(jnp.logical_and(z == 0, c == 0))
    def _():
        ext[pl.ds(1, TAPS - 1), :] = prior_ref[...].astype(F32)

    ext[pl.ds(TAPS, ROWS), :] = kvp[...].astype(F32)
    ext[pl.ds(TAPS + ROWS, 8), :] = jnp.zeros((8, WID), F32)
    total = TAPS + ROWS
    for r in range(8):
        shifts[r] = ext[r : r + total, :]

    half = ROWS // 2

    def conv_part(rows, lanes):
        def step(a, tot):
            base = pl.multiple_of(a * 8, 8)
            coeffs = table[pl.ds(base, 8), lanes]
            for r in range(8):
                window = shifts[r, pl.ds(pl.multiple_of(base + rows, 8), half), lanes]
                tot = tot + coeffs[r : r + 1] * window
            return tot

        conv = lax.fori_loop(0, TAPS // 8 + 1, step, jnp.zeros((half, HD), F32))
        out = (hy_ref[0, rows : rows + half, lanes].astype(F32) * conv).astype(BF16)
        hbuf[c, me_i, rows : rows + half, lanes] = out

    conv_part(0, slice(0, HD))
    serve(1)
    conv_part(0, slice(HD, WID))
    serve(1)
    conv_part(half, slice(0, HD))
    serve(1)
    conv_part(half, slice(HD, WID))

    quarter = half // 2

    def slot(ex, ey):
        return lax.rem(x - ex + NX, NX) * NY + lax.rem(y - ey + NY, NY)

    def spread_over(block, row, plus, minus, ss, rs):
        def send(e, at, size, to, code):
            ref = hbuf.at[c, block(e), pl.ds(row + at, size)]
            return remote(ref, ref, ss(code), rs(code), to)

        return {
            1: send(0, 0, half, plus, 1),
            3: send(0, 0, half, minus, 3),
            2: send(1, 0, quarter, plus, 2),
            0: send(3, quarter, quarter, minus, 0),
        }

    def at_x(e):
        return slot(e, 0)

    def at_y(e):
        return slot(0, e)

    xs = dev(z, c, x + 1, y), dev(z, c, x - 1, y)
    ys = dev(z, c, x, y + 1), dev(z, c, x, y - 1)
    one = [
        lambda: spread_over(at_x, 0, *xs, lambda n: a1_s.at[n], lambda n: a1_r.at[n]),
        lambda: spread_over(at_y, half, *ys, lambda n: b1_s.at[n], lambda n: b1_r.at[n]),
    ]
    two = [
        lambda o: spread_over(lambda e: slot(o, e), 0, *ys, lambda n: a2_s.at[o, n], lambda n: a2_r.at[o, n]),
        lambda o: spread_over(lambda e: slot(e, o), half, *xs, lambda n: b2_s.at[o, n], lambda n: b2_r.at[o, n]),
    ]

    def start_both(copies):
        copies[1].start()
        copies[3].start()

    def pass_on(copies):
        copies[1].wait_recv()
        copies[2].start()
        copies[3].wait_recv()
        copies[0].start()

    def last_of(copies):
        copies[2].wait_recv()
        copies[0].wait_recv()

    def to_sib(ex, ey):
        ref = hbuf.at[c, slot(ex, ey)]
        return remote(ref, ref, hs_s.at[ex, ey], hs_r.at[ex, ey], sib)

    for copies in one:
        start_both(copies())
    for copies in two:
        start_both(copies(0))
    to_sib(0, 0).start()
    serve(5)
    for n in range(2):
        pass_on(one[n]())
        start_both(two[n](1))
        start_both(two[n](3))
    serve(3)
    for n in range(2):
        last_of(one[n]())
        start_both(two[n](2))
    for n in range(2):
        pass_on(two[n](0))
    serve(3)
    for o in (1, 3):
        for n in range(2):
            pass_on(two[n](o))
        serve(2)
    for key in ((1, 0), (3, 0), (0, 1), (0, 3), (1, 1), (1, 3), (3, 1), (3, 3)):
        to_sib(*key).start()
    for n in range(2):
        last_of(two[n](0))
        pass_on(two[n](2))
    to_sib(2, 0).start()
    to_sib(0, 2).start()
    serve(2)
    for o in (1, 3):
        for n in range(2):
            last_of(two[n](o))
        for key in ((o, 2), (2, o)):
            to_sib(*key).start()
    serve(2)
    for n in range(2):
        last_of(two[n](2))
    to_sib(2, 2).start()
    for n, (ref, buf) in enumerate(((ck_ref, kold), (cv_ref, vold))):
        csibs[n].wait_recv()
        both = [ref[:, mine].astype(F32), csib[n].astype(F32)]
        buf[...] = jnp.concatenate(both, axis=0).astype(BF16)
    serve(2)

    ssq[...] = jnp.zeros_like(ssq)

    def squares(h, i):
        blk = hbuf[h, i].astype(F32)
        sq = blk * blk
        ssq[pl.ds(pl.multiple_of(h * ROWS, ROWS), ROWS), :] += sq[:, :HD] + sq[:, HD:]

    @pl.loop(0, NX * NY)
    def _(i):
        squares(c, i)

    @pl.loop(0, NX * NY)
    def _(n):
        ex, ey = n // NY, lax.rem(n, NY)
        to_sib(ex, ey).wait_recv()
        squares(1 - c, slot(ex, ey))

    inv = lax.rsqrt(jnp.sum(ssq[...], axis=1, keepdims=True) * (1.0 / D) + EPS)
    ssq[...] = jnp.broadcast_to(inv, ssq.shape)
    serve(2)

    def project(i, first=False):
        ga, gb = gain_ref[pl.ds(2 * i, 1), :], gain_ref[pl.ds(2 * i + 1, 1), :]
        g = jnp.concatenate([ga, gb], axis=1)
        for h in range(2):
            rows = pl.ds(h * ROWS, ROWS)
            scale = ssq[rows, :]
            scale = jnp.concatenate([scale, scale], axis=1)
            normed = (hbuf[h, i].astype(F32) * scale * g).astype(BF16)
            product = jnp.dot(normed, wbuf[i], preferred_element_type=F32)
            acc[rows, :] = product if first else acc[rows, :] + product

    def arrived(k):
        project(lax.rem(z + k, NZ))
        project(lax.rem(z - k + NZ, NZ))

    project(z, True)
    arrived(1)
    serve(1)
    arrived(2)
    arrived(3)
    serve(1)
    arrived(4)
    arrived(5)
    serve(1)
    arrived(6)
    serve(1)
    arrived(7)
    serve(2)
    assert served[0] == SUB * NZ // 2
    project(lax.rem(z + NZ // 2, NZ))

    qbuf[z] = acc[:, :HD].astype(BF16)
    knew[...] = acc[:, HD : 2 * HD].astype(BF16)
    vnew[...] = acc[:, 2 * HD :].astype(BF16)

    def at(way, k, h):
        return (way * 8 + k - 1) * 2 + h

    def piece_at(way, k, j):
        return (way * 8 + k - 1) * SUB + j

    def rows_of(h):
        return pl.ds(pl.multiple_of(h * ROWS, ROWS), ROWS)

    def source(way, k):
        return lax.rem(z + (2 * way - 1) * k + NZ, NZ)

    def along(way):
        return dev(z + 1 - 2 * way, c, x, y)

    def query(way, k, j):
        ref = qbuf.at[source(way, k - 1), pl.ds(pl.multiple_of(j * HB, HB), HB)]
        n = piece_at(way, k, j)
        return remote(ref, ref, q_s.at[n], q_r.at[n], along(way))

    def scores(q, keys):
        s = lax.dot_general(q, keys, (((1,), (1,)), ((), ())), preferred_element_type=F32)
        return s * SCALE

    def part(slot, pairs):
        m = pairs[0][0].max(axis=1, keepdims=True)
        for s, _ in pairs[1:]:
            m = jnp.maximum(m, s.max(axis=1, keepdims=True))
        o = l = None
        for s, vals in pairs:
            p = jnp.exp2(s - m)
            a = jnp.dot(p.astype(BF16), vals[...], preferred_element_type=F32)
            b = p.sum(axis=1, keepdims=True)
            o, l = (a, b) if o is None else (o + a, l + b)
        po[slot] = o
        pm[slot] = jnp.broadcast_to(m, (ROWS, HD))
        ps[slot] = jnp.broadcast_to(l, (ROWS, HD))

    def visit(way, k, h):
        slot = at(way, k, h)
        src = source(way, k)

        @pl.when(src > z)
        def _():
            q = qbuf[src, rows_of(h)]
            part(slot, [(scores(q, knew[...]), vnew), (scores(q, kold[...]), vold)])

        @pl.when(src < z)
        def _():
            q = qbuf[src, rows_of(h)]
            part(slot, [(scores(q, kold[...]), vold)])

    for j in range(SUB):
        for way in range(2):
            query(way, 1, j).start()

    @pl.loop(0, 2)
    def _(h):
        q = qbuf[z, rows_of(h)]
        s = scores(q, knew[...])
        t = h * ROWS + lax.broadcasted_iota(jnp.int32, s.shape, 0)
        s = jnp.where(lax.broadcasted_iota(jnp.int32, s.shape, 1) <= t, s, -1e30)
        part(32 + h, [(s, vnew), (scores(q, kold[...]), vold)])

    def merged(slot, rows, msg):
        msg_m = jnp.transpose(jnp.broadcast_to(tin[msg, 0:1], (HD, HB)))
        msg_s = jnp.transpose(jnp.broadcast_to(tin[msg, 4:5], (HD, HB)))
        own_m = pm[slot, rows]
        m = jnp.maximum(own_m, msg_m)
        mine_f = jnp.exp2(own_m - m)
        msg_f = jnp.exp2(msg_m - m)
        o = po[slot, rows] * mine_f + oin[msg].astype(F32) * msg_f
        return o, m, ps[slot, rows] * mine_f + msg_s * msg_f

    def answer(way, k, j):
        n = piece_at(way, k, j)
        to = along(1 - way)
        return (
            remote(osend.at[n], oin.at[n], o_s.at[n], o_r.at[n], to),
            remote(tsend.at[n], tin.at[n], t_s.at[n], t_r.at[n], to),
        )

    def arrive(way, k, j):
        for cp in answer(way, k + 1, j):
            cp.wait_recv()

    def rows_in(j):
        return pl.ds(pl.multiple_of(lax.rem(j, 2) * HB, HB), HB)

    def give(way, k, j, last):
        slot, rows, n = at(way, k, j // 2), rows_in(j), piece_at(way, k, j)
        if last:
            o, m, l = po[slot, rows], pm[slot, rows], ps[slot, rows]
        else:
            arrive(way, k, j)
            o, m, l = merged(slot, rows, piece_at(way, k + 1, j))
        osend[n] = o.astype(BF16)
        lane = lax.broadcasted_iota(jnp.int32, (HB, HD), 1)
        tsend[n] = jnp.transpose(jnp.where(lax.rem(lane, 8) < 4, m, l))[:8]
        for cp in answer(way, k, j):
            cp.start()

    @pl.loop(0, 12)
    def _(n):
        k, h = n // 2 + 1, lax.rem(n, 2)
        for jj in range(2):
            for way in range(2):
                query(way, k, 2 * h + jj).wait_recv()
                query(way, k + 1, 2 * h + jj).start()

        @pl.loop(0, 2)
        def _(way):
            visit(way, k, h)

    @pl.loop(0, 2)
    def _(way):
        for jj in range(2):
            query(way, 7, 2 * way + jj).wait_recv()
            query(way, 8, 2 * way + jj).start()

    @pl.loop(0, 2)
    def _(way):
        for jj in range(2):
            query(way, 7, 2 * (1 - way) + jj).wait_recv()
        visit(way, 7, 1 - way)
        for jj in range(2):
            give(way, 7, 2 * (1 - way) + jj, True)

    @pl.loop(0, 2)
    def _(way):
        for jj in range(2):
            query(way, 8, 2 * way + jj).wait_recv()
        visit(way, 8, way)
        for jj in range(2):
            give(way, 8, 2 * way + jj, True)

    @pl.loop(0, 2)
    def _(way):
        visit(way, 7, way)

    @pl.loop(0, 4)
    def _(n):
        way = lax.rem(n, 2)
        give(way, 7, 2 * way + n // 2, False)

    @pl.loop(0, 48)
    def _(n):
        k, p = 6 - n // 8, lax.rem(n // 2, 4)
        way = lax.rem(n, 2)
        give(way, k, lax.rem(p + 2 * (1 - way), SUB), False)

    def finish(h):
        slot = 32 + h
        for way in range(2):
            for jj in range(2):
                j = 2 * h + jj
                rows = pl.ds(jj * HB, HB)
                arrive(way, 0, j)
                o, m, l = merged(slot, rows, piece_at(way, 1, j))
                po[slot, rows], pm[slot, rows], ps[slot, rows] = o, m, l
        return (po[slot] / ps[slot]).astype(BF16)

    oswap[0] = finish(1 - c)
    swap = remote(oswap.at[0], oswap.at[1], x_s, x_r, sib)
    swap.start()
    out_ref[:, mine] = finish(c)
    swap.wait_recv()
    out_ref[:, theirs] = oswap[1]

    swap.wait_send()

    @pl.loop(0, 60)
    def _(n):
        k, way = n // 8 + 1, lax.rem(n, 2)
        j = lax.rem(n // 2, 4)
        j = jnp.where(n < 56, j, 2 * way + j)
        query(way, k, j).wait_send()
        for cp in answer(way, k, j):
            cp.wait_send()

    for cp in csibs:
        cp.wait_send()
    wsib.wait_send()
    hcopy.wait_send()

    @pl.loop(0, SUB * (NZ // 2 - 1))
    def _(n):
        for way in range(2):
            weight(way, n // SUB + 1, lax.rem(n, SUB)).wait_send()

    for j in range(SUB):
        weight(2 * j // SUB, NZ // 2, j).wait_send()
    for copies in one:
        for cp in copies().values():
            cp.wait_send()

    @pl.loop(0, 4)
    def _(o):
        for copies in two:
            for cp in copies(o).values():
                cp.wait_send()

    @pl.loop(0, NX * NY)
    def _(n):
        to_sib(n // NY, lax.rem(n, NY)).wait_send()


def body(hyena_in, prior_kv, filters, gain, w_qkv, cache_k, cache_v):
    hy = jnp.transpose(hyena_in, (1, 0, 2))
    w = jnp.transpose(w_qkv, (1, 0, 2))
    g = gain.reshape(D // HD, HD)
    old = cache_k.shape[0]
    dma = pltpu.SemaphoreType.DMA
    vmem = pltpu.VMEM
    return pl.pallas_call(
        whole_kernel,
        name="whole",
        out_shape=jax.ShapeDtypeStruct((ROWS, WID), BF16),
        in_specs=[pl.BlockSpec(memory_space=pltpu.VMEM)] * 7,
        out_specs=pl.BlockSpec(memory_space=pltpu.VMEM),
        scratch_shapes=[
            vmem((HD, 3 * HD), BF16),
            vmem((NZ, WID, 3 * HD), BF16),
            vmem((ROWS, WID), BF16),
            vmem((TAPS, WID), BF16),
            vmem((TAPS + ROWS + 8, WID), F32),
            vmem((8, TAPS + ROWS, WID), F32),
            vmem((136, WID), F32),
            vmem((2, NX * NY, ROWS, WID), BF16),
            vmem((2 * ROWS, 3 * HD), F32),
            vmem((2 * ROWS, HD), F32),
            dma, dma, dma, dma,
            dma((32,)), dma((32,)), dma((32,)), dma((32,)),
            dma((4,)), dma((4,)), dma((4,)), dma((4,)),
            dma((4, 4)), dma((4, 4)), dma((4, 4)), dma((4, 4)),
            dma((4, 4)), dma((4, 4)),
            vmem((2, old, HD), BF16),
            vmem((2 * old, HD), BF16),
            vmem((2 * old, HD), BF16),
            vmem((2 * ROWS, HD), BF16),
            vmem((2 * ROWS, HD), BF16),
            vmem((NZ, 2 * ROWS, HD), BF16),
            vmem((34, ROWS, HD), F32),
            vmem((34, ROWS, HD), F32),
            vmem((34, ROWS, HD), F32),
            vmem((64, HB, HD), BF16),
            vmem((64, HB, HD), BF16),
            vmem((64, 8, HB), F32),
            vmem((64, 8, HB), F32),
            vmem((2, ROWS, HD), BF16),
            dma((2,)), dma((2,)),
            dma((64,)), dma((64,)), dma((64,)), dma((64,)), dma((64,)), dma((64,)),
            dma, dma,
        ],
        compiler_params=pltpu.CompilerParams(
            collective_id=1, has_side_effects=True, vmem_limit_bytes=56 * 1024 * 1024
        ),
    )(hy, prior_kv, filters, g, w, cache_k, cache_v)


def solution(mesh):
    return jax.shard_map(
        body,
        mesh=mesh,
        in_specs=(
            P("seq", None, "chan"),
            P(None, "chan"),
            P("chan", None),
            P(),
            P("seq", None, "chan"),
            P("seq", "chan"),
            P("seq", "chan"),
        ),
        out_specs=P("seq", "chan"),
        check_vma=False,
    )
```

```python
import jax
import jax.numpy as jnp
from jax import lax
from jax.experimental import pallas as pl
from jax.experimental.pallas import tpu as pltpu
from jax.sharding import PartitionSpec as P

MESH = pl.DeviceIdType.MESH
F32 = jnp.float32
BF16 = jnp.bfloat16
NZ = 16
NX = 4
NY = 4
ROWS = 256
WID = 256
HD = 128
TAPS = 128
D = NX * NY * WID
EPS = 1e-6
FAR = 4
SUB = 4
HB = 2 * ROWS // SUB
SCALE = 1.4426950408889634 / HD**0.5


def place():
    s = lax.axis_index("seq")
    i = lax.axis_index("chan")
    return s // 2, lax.rem(s, 2), i // NY, lax.rem(i, NY)


def dev(z, c, x, y):
    return (lax.rem(z + NZ, NZ) * 2 + c, lax.rem(x + NX, NX) * NY + lax.rem(y + NY, NY))


def whole_kernel(
    hy_ref, prior_ref, filt_ref, gain_ref, w_ref, ck_ref, cv_ref, out_ref,
    wsend, wbuf, kvp, halo, ext, shifts, table, hbuf, acc, ssq,
    sib_s, sib_r, halo_s, halo_r, up_s, up_r, dn_s, dn_r,
    a1_s, a1_r, b1_s, b1_r, a2_s, a2_r, b2_s, b2_r, hs_s, hs_r,
    csib, kold, vold, knew, vnew, qbuf, po, pt, osend, oin, tsend, tin, oswap,
    cs_s, cs_r, e_s, e_r, q_s, q_r, o_s, o_r, t_s, t_r, x_s, x_r,
):
    z, c, x, y = place()
    me_i = x * NY + y
    sib = dev(z, 1 - c, x, y)
    above = dev(z + 1, c, x, y)
    below = dev(z - 1, c, x, y)
    nxt = dev(z + c, 1 - c, x, y)
    other = dev(z + 2 * c - 1, 1 - c, x, y)

    def remote(src, dst, ss, rs, to):
        return pltpu.make_async_remote_copy(
            src_ref=src, dst_ref=dst, send_sem=ss, recv_sem=rs, device_id=to, device_id_type=MESH
        )

    barrier = pltpu.get_barrier_semaphore()
    par = lax.rem(z, 2)
    twin = dev(z + 1 - 2 * par, c, x, y)
    partners = [sib, above, below, other, dev(z + 2, c, x, y), dev(z - 2, c, x, y)]
    partners += [dev(z, c, x + d, y) for d in (1, -1)]
    partners += [dev(z, c, x, y + d) for d in (1, -1)]
    for to in partners:
        pl.semaphore_signal(barrier, inc=1, device_id=to, device_id_type=MESH)

    mine = pl.ds(pl.multiple_of(c * HD, HD), HD)
    theirs = pl.ds(pl.multiple_of((1 - c) * HD, HD), HD)
    for j in range(3):
        wbuf[z, mine, j * HD : (j + 1) * HD] = w_ref[j, :, mine]
        wsend[:, j * HD : (j + 1) * HD] = w_ref[j, :, theirs]
    kvp[...] = (hy_ref[1].astype(F32) * hy_ref[2].astype(F32)).astype(BF16)
    pl.semaphore_wait(barrier, len(partners))

    wsib = remote(wsend, wbuf.at[z, mine, :], sib_s, sib_r, sib)
    wsib.start()
    csibs = [
        remote(ref.at[:, theirs], csib.at[n], cs_s.at[n], cs_r.at[n], sib)
        for n, ref in enumerate((ck_ref, cv_ref))
    ]
    for cp in csibs:
        cp.start()
    hcopy = remote(kvp.at[pl.ds(ROWS - TAPS, TAPS)], halo, halo_s, halo_r, nxt)
    hcopy.start()

    def goes(way, k, j):
        return k < NZ // 2 or (k == NZ // 2 and (j < SUB // 2) == (way == 0))

    def weight(way, k, j):
        src = lax.rem(z + (2 * way - 1) * (k - 1) + NZ, NZ)
        ref = wbuf.at[src, pl.ds(pl.multiple_of(j * (WID // SUB), WID // SUB), WID // SUB)]
        n = (k - 1) * SUB + j
        ss, rs = (up_s, up_r) if way == 0 else (dn_s, dn_r)
        return remote(ref, ref, ss.at[n], rs.at[n], (above, below)[way])

    def ring_next(n):
        k, j = n // SUB + 1, n % SUB
        for way in range(2):
            if goes(way, k, j):
                weight(way, k, j).wait_recv()
            if goes(way, k + 1, j):
                weight(way, k + 1, j).start()

    served = [0]

    def serve(count):
        begin, end = served[0], served[0] + count
        served[0] = end
        looped = min(end, SUB * (NZ // 2 - 2))
        if looped - begin > 1:

            @pl.loop(begin, looped)
            def _(n):
                k, j = n // SUB + 1, lax.rem(n, SUB)
                for way in range(2):
                    weight(way, k, j).wait_recv()
                    weight(way, k + 1, j).start()

            begin = looped
        for n in range(begin, end):
            ring_next(n)

    rev = (
        lax.broadcasted_iota(jnp.int32, (136, TAPS), 0)
        + lax.broadcasted_iota(jnp.int32, (136, TAPS), 1)
        == TAPS
    ).astype(F32)
    groups = filt_ref.shape[0]
    spread = (
        lax.broadcasted_iota(jnp.int32, (groups, WID), 0)
        == lax.broadcasted_iota(jnp.int32, (groups, WID), 1) // (WID // groups)
    ).astype(F32)
    reversed_taps = lax.dot_general(
        rev, filt_ref[...], (((1,), (1,)), ((), ())),
        precision=lax.Precision.HIGHEST, preferred_element_type=F32,
    )
    table[...] = lax.dot_general(
        reversed_taps, spread, (((1,), (0,)), ((), ())),
        precision=lax.Precision.HIGHEST, preferred_element_type=F32,
    )

    wsib.wait_recv()
    for j in range(SUB):
        for way in range(2):
            weight(way, 1, j).start()
    hcopy.wait_recv()

    ext[pl.ds(0, TAPS), :] = halo[...].astype(F32)

    @pl.when(jnp.logical_and(z == 0, c == 0))
    def _():
        ext[pl.ds(1, TAPS - 1), :] = prior_ref[...].astype(F32)

    ext[pl.ds(TAPS, ROWS), :] = kvp[...].astype(F32)
    ext[pl.ds(TAPS + ROWS, 8), :] = jnp.zeros((8, WID), F32)
    total = TAPS + ROWS
    for r in range(8):
        shifts[r] = ext[r : r + total, :]

    half = ROWS // 2

    def conv_part(rows, lanes):
        def step(a, tot):
            base = pl.multiple_of(a * 8, 8)
            coeffs = table[pl.ds(base, 8), lanes]
            for r in range(8):
                window = shifts[r, pl.ds(pl.multiple_of(base + rows, 8), half), lanes]
                tot = tot + coeffs[r : r + 1] * window
            return tot

        conv = lax.fori_loop(0, TAPS // 8 + 1, step, jnp.zeros((half, HD), F32))
        out = (hy_ref[0, rows : rows + half, lanes].astype(F32) * conv).astype(BF16)
        hbuf[c, me_i, rows : rows + half, lanes] = out

    conv_part(0, slice(0, HD))
    serve(1)
    conv_part(0, slice(HD, WID))
    serve(1)
    conv_part(half, slice(0, HD))
    serve(1)
    conv_part(half, slice(HD, WID))

    quarter = half // 2

    def slot(ex, ey):
        return lax.rem(x - ex + NX, NX) * NY + lax.rem(y - ey + NY, NY)

    def spread_over(block, row, plus, minus, ss, rs):
        def send(e, at, size, to, code):
            ref = hbuf.at[c, block(e), pl.ds(row + at, size)]
            return remote(ref, ref, ss(code), rs(code), to)

        return {
            1: send(0, 0, half, plus, 1),
            3: send(0, 0, half, minus, 3),
            2: send(1, 0, quarter, plus, 2),
            0: send(3, quarter, quarter, minus, 0),
        }

    def at_x(e):
        return slot(e, 0)

    def at_y(e):
        return slot(0, e)

    xs = dev(z, c, x + 1, y), dev(z, c, x - 1, y)
    ys = dev(z, c, x, y + 1), dev(z, c, x, y - 1)
    one = [
        lambda: spread_over(at_x, 0, *xs, lambda n: a1_s.at[n], lambda n: a1_r.at[n]),
        lambda: spread_over(at_y, half, *ys, lambda n: b1_s.at[n], lambda n: b1_r.at[n]),
    ]
    two = [
        lambda o: spread_over(lambda e: slot(o, e), 0, *ys, lambda n: a2_s.at[o, n], lambda n: a2_r.at[o, n]),
        lambda o: spread_over(lambda e: slot(e, o), half, *xs, lambda n: b2_s.at[o, n], lambda n: b2_r.at[o, n]),
    ]

    def start_both(copies):
        copies[1].start()
        copies[3].start()

    def pass_on(copies):
        copies[1].wait_recv()
        copies[2].start()
        copies[3].wait_recv()
        copies[0].start()

    def last_of(copies):
        copies[2].wait_recv()
        copies[0].wait_recv()

    def to_sib(ex, ey):
        ref = hbuf.at[c, slot(ex, ey)]
        return remote(ref, ref, hs_s.at[ex, ey], hs_r.at[ex, ey], sib)

    for copies in one:
        start_both(copies())
    for copies in two:
        start_both(copies(0))
    to_sib(0, 0).start()
    serve(5)
    for n in range(2):
        pass_on(one[n]())
        start_both(two[n](1))
        start_both(two[n](3))
    serve(3)
    for n in range(2):
        last_of(one[n]())
        start_both(two[n](2))
    for n in range(2):
        pass_on(two[n](0))
    serve(3)
    for o in (1, 3):
        for n in range(2):
            pass_on(two[n](o))
        serve(2)
    for key in ((1, 0), (3, 0), (0, 1), (0, 3), (1, 1), (1, 3), (3, 1), (3, 3)):
        to_sib(*key).start()
    for n in range(2):
        last_of(two[n](0))
        pass_on(two[n](2))
    to_sib(2, 0).start()
    to_sib(0, 2).start()
    serve(2)
    for o in (1, 3):
        for n in range(2):
            last_of(two[n](o))
        for key in ((o, 2), (2, o)):
            to_sib(*key).start()
    serve(2)
    for n in range(2):
        last_of(two[n](2))
    to_sib(2, 2).start()
    def share(n):
        ref = (kold, vold, knew, vnew)[n].at[par]
        return remote(ref, ref, e_s.at[n], e_r.at[n], twin)

    for n, ref in enumerate((ck_ref, cv_ref)):
        csibs[n].wait_recv()
        both = jnp.concatenate([ref[:, mine].astype(F32), csib[n].astype(F32)], axis=0)
        if n == 0:
            kold[par] = both.astype(BF16)
        else:
            vold[par] = jnp.transpose(both).astype(BF16)
        share(n).start()
    serve(2)

    ssq[...] = jnp.zeros_like(ssq)

    def squares(h, i):
        blk = hbuf[h, i].astype(F32)
        sq = blk * blk
        ssq[pl.ds(pl.multiple_of(h * ROWS, ROWS), ROWS), :] += sq[:, :HD] + sq[:, HD:]

    @pl.loop(0, NX * NY)
    def _(i):
        squares(c, i)

    @pl.loop(0, NX * NY)
    def _(n):
        ex, ey = n // NY, lax.rem(n, NY)
        to_sib(ex, ey).wait_recv()
        squares(1 - c, slot(ex, ey))

    inv = lax.rsqrt(jnp.sum(ssq[...], axis=1, keepdims=True) * (1.0 / D) + EPS)
    ssq[...] = jnp.broadcast_to(inv, ssq.shape)
    serve(2)

    def project(i, first=False):
        ga, gb = gain_ref[pl.ds(2 * i, 1), :], gain_ref[pl.ds(2 * i + 1, 1), :]
        g = jnp.concatenate([ga, gb], axis=1)
        for h in range(2):
            rows = pl.ds(h * ROWS, ROWS)
            scale = ssq[rows, :]
            scale = jnp.concatenate([scale, scale], axis=1)
            normed = (hbuf[h, i].astype(F32) * scale * g).astype(BF16)
            product = jnp.dot(normed, wbuf[i], preferred_element_type=F32)
            acc[rows, :] = product if first else acc[rows, :] + product

    def arrived(k):
        project(lax.rem(z + k, NZ))
        project(lax.rem(z - k + NZ, NZ))

    project(z, True)
    arrived(1)
    serve(1)
    arrived(2)
    arrived(3)
    serve(1)
    arrived(4)
    arrived(5)
    serve(1)
    arrived(6)
    serve(1)
    arrived(7)
    serve(2)
    assert served[0] == SUB * NZ // 2
    project(lax.rem(z + NZ // 2, NZ))

    qbuf[z] = acc[:, :HD].astype(BF16)

    def at(way, k, h):
        return (way * FAR + k - 1) * 2 + h

    def piece_at(way, k, j):
        return (way * FAR + k - 1) * SUB + j

    def rows_of(h):
        return pl.ds(pl.multiple_of(h * ROWS, ROWS), ROWS)

    def source(way, k):
        return lax.rem(z + (4 * way - 2) * k + NZ, NZ)

    def along(way):
        return dev(z + 2 - 4 * way, c, x, y)

    def query(way, k, j):
        ref = qbuf.at[source(way, k - 1), pl.ds(pl.multiple_of(j * HB, HB), HB)]
        n = piece_at(way, k, j)
        return remote(ref, ref, q_s.at[n], q_r.at[n], along(way))

    def scores(q, keys):
        s = lax.dot_general(keys, q, (((1,), (1,)), ((), ())), preferred_element_type=F32)
        return s * SCALE

    def part(slot, pairs):
        m = pairs[0][0].max(axis=0, keepdims=True)
        for s, _ in pairs[1:]:
            m = jnp.maximum(m, s.max(axis=0, keepdims=True))
        o = l = None
        for s, vals in pairs:
            p = jnp.exp2(s - m)
            a = jnp.dot(vals[...], p.astype(BF16), preferred_element_type=F32)
            b = p.sum(axis=0, keepdims=True)
            o, l = (a, b) if o is None else (o + a, l + b)
        po[slot] = o
        pt[slot, 0:1] = m
        pt[slot, 1:2] = l

    def old(q):
        return [(scores(q, kold[n]), vold.at[n]) for n in range(2)]

    def new(q, n):
        return scores(q, knew[n]), vnew.at[n]

    def visit(way, k, h):
        slot = at(way, k, h)
        src = source(way, k)

        @pl.when(src > z)
        def _():
            q = qbuf[src, rows_of(h)]
            part(slot, [new(q, 0), new(q, 1)] + old(q))

        @pl.when(src < z)
        def _():
            q = qbuf[src, rows_of(h)]
            part(slot, old(q))

    for j in range(SUB):
        for way in range(2):
            query(way, 1, j).start()
    knew[par] = acc[:, HD : 2 * HD].astype(BF16)
    share(2).start()
    vnew[par] = jnp.transpose(acc[:, 2 * HD :]).astype(BF16)
    share(3).start()

    def own(h, earlier):
        q = qbuf[z, rows_of(h)]
        s, vals = new(q, par)
        t = h * ROWS + lax.broadcasted_iota(jnp.int32, s.shape, 1)
        s = jnp.where(lax.broadcasted_iota(jnp.int32, s.shape, 0) <= t, s, -1e30)
        part(4 * FAR + h, [(s, vals)] + earlier(q) + old(q))

    def merged(slot, cols, msg):
        own_m, msg_m = pt[slot, 0:1, cols], tin[msg, 0:1]
        m = jnp.maximum(own_m, msg_m)
        own_f = jnp.exp2(own_m - m)
        msg_f = jnp.exp2(msg_m - m)
        o = po[slot, :, cols] * own_f + oin[msg].astype(F32) * msg_f
        return o, m, pt[slot, 1:2, cols] * own_f + tin[msg, 1:2] * msg_f

    def answer(way, k, j):
        n = piece_at(way, k, j)
        to = along(1 - way)
        return (
            remote(osend.at[n], oin.at[n], o_s.at[n], o_r.at[n], to),
            remote(tsend.at[n], tin.at[n], t_s.at[n], t_r.at[n], to),
        )

    def arrive(way, k, j):
        for cp in answer(way, k + 1, j):
            cp.wait_recv()

    def cols_in(j):
        return pl.ds(pl.multiple_of(lax.rem(j, 2) * HB, HB), HB)

    def give(last, *steps):
        if not last:
            for step in steps:
                arrive(*step)
        for way, k, j in steps:
            slot, cols, n = at(way, k, j // 2), cols_in(j), piece_at(way, k, j)
            if last:
                o, m, l = po[slot, :, cols], pt[slot, 0:1, cols], pt[slot, 1:2, cols]
            else:
                o, m, l = merged(slot, cols, piece_at(way, k + 1, j))
            osend[n] = o.astype(BF16)
            tsend[n, 0:1] = m
            tsend[n, 1:2] = l
        for step in steps:
            for cp in answer(*step):
                cp.start()

    def service(k, h):
        for jj in range(2):
            for way in range(2):
                query(way, k, 2 * h + jj).wait_recv()
                query(way, k + 1, 2 * h + jj).start()

    def visits(k, h):
        @pl.loop(0, 2)
        def _(way):
            visit(way, k, h)

    @pl.loop(0, 2)
    def _(h):
        service(1, h)

    for n in range(4):
        share(n).wait_recv()

    @pl.when(par == 0)
    def _():
        @pl.loop(0, 2)
        def _(h):
            own(h, lambda q: [])

    @pl.when(par == 1)
    def _():
        @pl.loop(0, 2)
        def _(h):
            own(h, lambda q: [new(q, 0)])

    @pl.loop(0, 2)
    def _(h):
        service(2, h)
        visits(1, h)

    @pl.loop(0, 2)
    def _(h):
        for jj in range(2):
            for way in range(2):
                query(way, FAR - 1, 2 * h + jj).wait_recv()
            query(h, FAR, 2 * h + jj).start()
        visits(2, h)

    @pl.loop(0, 2)
    def _(way):
        visit(way, FAR - 1, 1 - way)
        for jj in range(2):
            give(True, (way, FAR - 1, 2 * (1 - way) + jj))

    @pl.loop(0, 2)
    def _(way):
        for jj in range(2):
            query(way, FAR, 2 * way + jj).wait_recv()
        visit(way, FAR, way)
        for jj in range(2):
            give(True, (way, FAR, 2 * way + jj))

    @pl.loop(0, 2)
    def _(way):
        visit(way, FAR - 1, way)

    @pl.loop(0, 2)
    def _(n):
        give(False, (0, FAR - 1, n), (1, FAR - 1, 2 + n))

    @pl.loop(0, SUB * (FAR - 2))
    def _(n):
        k, p = FAR - 2 - n // SUB, lax.rem(n, SUB)
        give(False, (0, k, lax.rem(p + 2, SUB)), (1, k, p))

    def finish(h):
        slot = 4 * FAR + h
        for jj in range(2):
            cols = pl.ds(jj * HB, HB)
            for way in range(2):
                j = 2 * h + jj
                arrive(way, 0, j)
                o, m, l = merged(slot, cols, piece_at(way, 1, j))
                po[slot, :, cols] = o
                pt[slot, 0:1, cols] = m
                pt[slot, 1:2, cols] = l
        return jnp.transpose(po[slot] / pt[slot, 1:2]).astype(BF16)

    oswap[0] = finish(1 - c)
    swap = remote(oswap.at[0], oswap.at[1], x_s, x_r, sib)
    swap.start()
    out_ref[:, mine] = finish(c)
    swap.wait_recv()
    out_ref[:, theirs] = oswap[1]

    swap.wait_send()

    @pl.loop(0, 8 * FAR - 4)
    def _(n):
        k, way = n // 8 + 1, lax.rem(n, 2)
        j = lax.rem(n // 2, SUB)
        j = jnp.where(k < FAR, j, 2 * way + j)
        query(way, k, j).wait_send()
        for cp in answer(way, k, j):
            cp.wait_send()

    for n in range(4):
        share(n).wait_send()
    for cp in csibs:
        cp.wait_send()
    wsib.wait_send()
    hcopy.wait_send()

    @pl.loop(0, SUB * (NZ // 2 - 1))
    def _(n):
        for way in range(2):
            weight(way, n // SUB + 1, lax.rem(n, SUB)).wait_send()

    for j in range(SUB):
        weight(2 * j // SUB, NZ // 2, j).wait_send()
    for copies in one:
        for cp in copies().values():
            cp.wait_send()

    @pl.loop(0, 4)
    def _(o):
        for copies in two:
            for cp in copies(o).values():
                cp.wait_send()

    @pl.loop(0, NX * NY)
    def _(n):
        to_sib(n // NY, lax.rem(n, NY)).wait_send()


def body(hyena_in, prior_kv, filters, gain, w_qkv, cache_k, cache_v):
    hy = jnp.transpose(hyena_in, (1, 0, 2))
    w = jnp.transpose(w_qkv, (1, 0, 2))
    g = gain.reshape(D // HD, HD)
    old = cache_k.shape[0]
    dma = pltpu.SemaphoreType.DMA
    vmem = pltpu.VMEM
    return pl.pallas_call(
        whole_kernel,
        name="whole",
        out_shape=jax.ShapeDtypeStruct((ROWS, WID), BF16),
        in_specs=[pl.BlockSpec(memory_space=pltpu.VMEM)] * 7,
        out_specs=pl.BlockSpec(memory_space=pltpu.VMEM),
        scratch_shapes=[
            vmem((HD, 3 * HD), BF16),
            vmem((NZ, WID, 3 * HD), BF16),
            vmem((ROWS, WID), BF16),
            vmem((TAPS, WID), BF16),
            vmem((TAPS + ROWS + 8, WID), F32),
            vmem((8, TAPS + ROWS, WID), F32),
            vmem((136, WID), F32),
            vmem((2, NX * NY, ROWS, WID), BF16),
            vmem((2 * ROWS, 3 * HD), F32),
            vmem((2 * ROWS, HD), F32),
            dma, dma, dma, dma,
            dma((32,)), dma((32,)), dma((32,)), dma((32,)),
            dma((4,)), dma((4,)), dma((4,)), dma((4,)),
            dma((4, 4)), dma((4, 4)), dma((4, 4)), dma((4, 4)),
            dma((4, 4)), dma((4, 4)),
            vmem((2, old, HD), BF16),
            vmem((2, 2 * old, HD), BF16),
            vmem((2, HD, 2 * old), BF16),
            vmem((2, 2 * ROWS, HD), BF16),
            vmem((2, HD, 2 * ROWS), BF16),
            vmem((NZ, 2 * ROWS, HD), BF16),
            vmem((4 * FAR + 2, HD, ROWS), F32),
            vmem((4 * FAR + 2, 8, ROWS), F32),
            vmem((2 * FAR * SUB, HD, HB), BF16),
            vmem((2 * FAR * SUB, HD, HB), BF16),
            vmem((2 * FAR * SUB, 2, HB), F32),
            vmem((2 * FAR * SUB, 2, HB), F32),
            vmem((2, ROWS, HD), BF16),
            dma((2,)), dma((2,)), dma((4,)), dma((4,)),
            dma((32,)), dma((32,)), dma((32,)), dma((32,)), dma((32,)), dma((32,)),
            dma, dma,
        ],
        compiler_params=pltpu.CompilerParams(
            collective_id=1, has_side_effects=True, vmem_limit_bytes=56 * 1024 * 1024
        ),
    )(hy, prior_kv, filters, g, w, cache_k, cache_v)


def solution(mesh):
    return jax.shard_map(
        body,
        mesh=mesh,
        in_specs=(
            P("seq", None, "chan"),
            P(None, "chan"),
            P("chan", None),
            P(),
            P("seq", None, "chan"),
            P("seq", "chan"),
            P("seq", "chan"),
        ),
        out_specs=P("seq", "chan"),
        check_vma=False,
    )
```

```python
import jax
import jax.numpy as jnp
from jax import lax
from jax.experimental import pallas as pl
from jax.experimental.pallas import tpu as pltpu
from jax.sharding import PartitionSpec as P

MESH = pl.DeviceIdType.MESH
F32 = jnp.float32
BF16 = jnp.bfloat16
NZ = 16
NX = 4
NY = 4
ROWS = 256
WID = 256
HD = 128
TAPS = 128
D = NX * NY * WID
EPS = 1e-6
FAR = 4
SUB = 4
HB = 2 * ROWS // SUB
SCALE = 1.4426950408889634 / HD**0.5


def place():
    s = lax.axis_index("seq")
    i = lax.axis_index("chan")
    return s // 2, lax.rem(s, 2), i // NY, lax.rem(i, NY)


def dev(z, c, x, y):
    return (lax.rem(z + NZ, NZ) * 2 + c, lax.rem(x + NX, NX) * NY + lax.rem(y + NY, NY))


def whole_kernel(
    hy_ref, prior_ref, filt_ref, gain_ref, w_ref, ck_ref, cv_ref, out_ref,
    wsend, wbuf, kvp, halo, ext, shifts, table, hbuf, acc, ssq,
    sib_s, sib_r, halo_s, halo_r, up_s, up_r, dn_s, dn_r,
    a1_s, a1_r, b1_s, b1_r, a2_s, a2_r, b2_s, b2_r, hs_s, hs_r,
    csib, kold, vold, knew, vnew, qbuf, po, pt, osend, oin, tsend, tin, oswap,
    cs_s, cs_r, e_s, e_r, q_s, q_r, o_s, o_r, t_s, t_r, x_s, x_r,
):
    z, c, x, y = place()
    me_i = x * NY + y
    sib = dev(z, 1 - c, x, y)
    above = dev(z + 1, c, x, y)
    below = dev(z - 1, c, x, y)
    nxt = dev(z + c, 1 - c, x, y)
    other = dev(z + 2 * c - 1, 1 - c, x, y)

    def remote(src, dst, ss, rs, to):
        return pltpu.make_async_remote_copy(
            src_ref=src, dst_ref=dst, send_sem=ss, recv_sem=rs, device_id=to, device_id_type=MESH
        )

    barrier = pltpu.get_barrier_semaphore()
    par = lax.rem(z, 2)
    twin = dev(z + 1 - 2 * par, c, x, y)
    partners = [sib, above, below, other, dev(z + 2, c, x, y), dev(z - 2, c, x, y)]
    partners += [dev(z, c, x + d, y) for d in (1, -1)]
    partners += [dev(z, c, x, y + d) for d in (1, -1)]
    for to in partners:
        pl.semaphore_signal(barrier, inc=1, device_id=to, device_id_type=MESH)

    mine = pl.ds(pl.multiple_of(c * HD, HD), HD)
    theirs = pl.ds(pl.multiple_of((1 - c) * HD, HD), HD)
    for j in range(3):
        wbuf[z, mine, j * HD : (j + 1) * HD] = w_ref[j, :, mine]
        wsend[:, j * HD : (j + 1) * HD] = w_ref[j, :, theirs]
    kvp[...] = (hy_ref[1].astype(F32) * hy_ref[2].astype(F32)).astype(BF16)
    pl.semaphore_wait(barrier, len(partners))

    wsib = remote(wsend, wbuf.at[z, mine, :], sib_s, sib_r, sib)
    wsib.start()
    csibs = [
        remote(ref.at[:, theirs], csib.at[n], cs_s.at[n], cs_r.at[n], sib)
        for n, ref in enumerate((ck_ref, cv_ref))
    ]
    for cp in csibs:
        cp.start()
    hcopy = remote(kvp.at[pl.ds(ROWS - TAPS, TAPS)], halo, halo_s, halo_r, nxt)
    hcopy.start()

    def goes(way, k, j):
        return k < NZ // 2 or (k == NZ // 2 and (j < SUB // 2) == (way == 0))

    def weight(way, k, j):
        src = lax.rem(z + (2 * way - 1) * (k - 1) + NZ, NZ)
        row = lax.rem(j + c * (SUB // 2), SUB) * (WID // SUB)
        ref = wbuf.at[src, pl.ds(pl.multiple_of(row, WID // SUB), WID // SUB)]
        n = (k - 1) * SUB + j
        ss, rs = (up_s, up_r) if way == 0 else (dn_s, dn_r)
        return remote(ref, ref, ss.at[n], rs.at[n], (above, below)[way])

    for j in range(SUB // 2):
        for way in range(2):
            weight(way, 1, j).start()

    def ring_next(n):
        k, j = n // SUB + 1, n % SUB
        for way in range(2):
            if goes(way, k, j):
                weight(way, k, j).wait_recv()
            if goes(way, k + 1, j):
                weight(way, k + 1, j).start()

    served = [0]

    def serve(count):
        begin, end = served[0], served[0] + count
        served[0] = end
        looped = min(end, SUB * (NZ // 2 - 2))
        if looped - begin > 1:

            @pl.loop(begin, looped)
            def _(n):
                k, j = n // SUB + 1, lax.rem(n, SUB)
                for way in range(2):
                    weight(way, k, j).wait_recv()
                    weight(way, k + 1, j).start()

            begin = looped
        for n in range(begin, end):
            ring_next(n)

    rev = (
        lax.broadcasted_iota(jnp.int32, (136, TAPS), 0)
        + lax.broadcasted_iota(jnp.int32, (136, TAPS), 1)
        == TAPS
    ).astype(F32)
    groups = filt_ref.shape[0]
    spread = (
        lax.broadcasted_iota(jnp.int32, (groups, WID), 0)
        == lax.broadcasted_iota(jnp.int32, (groups, WID), 1) // (WID // groups)
    ).astype(F32)
    reversed_taps = lax.dot_general(
        rev, filt_ref[...], (((1,), (1,)), ((), ())),
        precision=lax.Precision.HIGHEST, preferred_element_type=F32,
    )
    table[...] = lax.dot_general(
        reversed_taps, spread, (((1,), (0,)), ((), ())),
        precision=lax.Precision.HIGHEST, preferred_element_type=F32,
    )

    wsib.wait_recv()
    for j in range(SUB // 2, SUB):
        for way in range(2):
            weight(way, 1, j).start()
    hcopy.wait_recv()

    ext[pl.ds(0, TAPS), :] = halo[...].astype(F32)

    @pl.when(jnp.logical_and(z == 0, c == 0))
    def _():
        ext[pl.ds(1, TAPS - 1), :] = prior_ref[...].astype(F32)

    ext[pl.ds(TAPS, ROWS), :] = kvp[...].astype(F32)
    ext[pl.ds(TAPS + ROWS, 8), :] = jnp.zeros((8, WID), F32)
    total = TAPS + ROWS
    for r in range(8):
        shifts[r] = ext[r : r + total, :]

    half = ROWS // 2

    def conv_part(rows, lanes):
        def step(a, tot):
            base = pl.multiple_of(a * 8, 8)
            coeffs = table[pl.ds(base, 8), lanes]
            for r in range(8):
                window = shifts[r, pl.ds(pl.multiple_of(base + rows, 8), half), lanes]
                tot = tot + coeffs[r : r + 1] * window
            return tot

        conv = lax.fori_loop(0, TAPS // 8 + 1, step, jnp.zeros((half, HD), F32))
        out = (hy_ref[0, rows : rows + half, lanes].astype(F32) * conv).astype(BF16)
        hbuf[c, me_i, rows : rows + half, lanes] = out

    conv_part(0, slice(0, HD))
    serve(1)
    conv_part(0, slice(HD, WID))
    serve(1)
    conv_part(half, slice(0, HD))
    serve(1)
    conv_part(half, slice(HD, WID))

    quarter = half // 2

    def slot(ex, ey):
        return lax.rem(x - ex + NX, NX) * NY + lax.rem(y - ey + NY, NY)

    def spread_over(block, row, plus, minus, ss, rs):
        def send(e, at, size, to, code):
            ref = hbuf.at[c, block(e), pl.ds(row + at, size)]
            return remote(ref, ref, ss(code), rs(code), to)

        return {
            1: send(0, 0, half, plus, 1),
            3: send(0, 0, half, minus, 3),
            2: send(1, 0, quarter, plus, 2),
            0: send(3, quarter, quarter, minus, 0),
        }

    def at_x(e):
        return slot(e, 0)

    def at_y(e):
        return slot(0, e)

    xs = dev(z, c, x + 1, y), dev(z, c, x - 1, y)
    ys = dev(z, c, x, y + 1), dev(z, c, x, y - 1)
    one = [
        lambda: spread_over(at_x, 0, *xs, lambda n: a1_s.at[n], lambda n: a1_r.at[n]),
        lambda: spread_over(at_y, half, *ys, lambda n: b1_s.at[n], lambda n: b1_r.at[n]),
    ]
    two = [
        lambda o: spread_over(lambda e: slot(o, e), 0, *ys, lambda n: a2_s.at[o, n], lambda n: a2_r.at[o, n]),
        lambda o: spread_over(lambda e: slot(e, o), half, *xs, lambda n: b2_s.at[o, n], lambda n: b2_r.at[o, n]),
    ]

    def start_both(copies):
        copies[1].start()
        copies[3].start()

    def pass_on(copies):
        copies[1].wait_recv()
        copies[2].start()
        copies[3].wait_recv()
        copies[0].start()

    def last_of(copies):
        copies[2].wait_recv()
        copies[0].wait_recv()

    def to_sib(ex, ey):
        ref = hbuf.at[c, slot(ex, ey)]
        return remote(ref, ref, hs_s.at[ex, ey], hs_r.at[ex, ey], sib)

    for copies in one:
        start_both(copies())
    for copies in two:
        start_both(copies(0))
    to_sib(0, 0).start()
    serve(5)
    for n in range(2):
        pass_on(one[n]())
        start_both(two[n](1))
        start_both(two[n](3))
    serve(3)
    for n in range(2):
        last_of(one[n]())
        start_both(two[n](2))
    for n in range(2):
        pass_on(two[n](0))
    serve(3)
    for o in (1, 3):
        for n in range(2):
            pass_on(two[n](o))
        serve(2)
    for key in ((1, 0), (3, 0), (0, 1), (0, 3), (1, 1), (1, 3), (3, 1), (3, 3)):
        to_sib(*key).start()
    for n in range(2):
        last_of(two[n](0))
        pass_on(two[n](2))
    to_sib(2, 0).start()
    to_sib(0, 2).start()
    serve(2)
    for o in (1, 3):
        for n in range(2):
            last_of(two[n](o))
        for key in ((o, 2), (2, o)):
            to_sib(*key).start()
    serve(2)
    for n in range(2):
        last_of(two[n](2))
    to_sib(2, 2).start()
    def share(n):
        ref = (kold, vold, knew, vnew)[n].at[par]
        return remote(ref, ref, e_s.at[n], e_r.at[n], twin)

    for n, ref in enumerate((ck_ref, cv_ref)):
        csibs[n].wait_recv()
        both = jnp.concatenate([ref[:, mine].astype(F32), csib[n].astype(F32)], axis=0)
        if n == 0:
            kold[par] = both.astype(BF16)
        else:
            vold[par] = jnp.transpose(both).astype(BF16)
        share(n).start()
    serve(2)

    ssq[...] = jnp.zeros_like(ssq)

    def squares(h, i):
        blk = hbuf[h, i].astype(F32)
        sq = blk * blk
        ssq[pl.ds(pl.multiple_of(h * ROWS, ROWS), ROWS), :] += sq[:, :HD] + sq[:, HD:]

    @pl.loop(0, NX * NY)
    def _(i):
        squares(c, i)

    @pl.loop(0, NX * NY)
    def _(n):
        ex, ey = n // NY, lax.rem(n, NY)
        to_sib(ex, ey).wait_recv()
        squares(1 - c, slot(ex, ey))

    inv = lax.rsqrt(jnp.sum(ssq[...], axis=1, keepdims=True) * (1.0 / D) + EPS)
    ssq[...] = jnp.broadcast_to(inv, ssq.shape)
    serve(2)

    def project(i, first=False):
        ga, gb = gain_ref[pl.ds(2 * i, 1), :], gain_ref[pl.ds(2 * i + 1, 1), :]
        g = jnp.concatenate([ga, gb], axis=1)
        for h in range(2):
            rows = pl.ds(h * ROWS, ROWS)
            scale = ssq[rows, :]
            scale = jnp.concatenate([scale, scale], axis=1)
            normed = (hbuf[h, i].astype(F32) * scale * g).astype(BF16)
            product = jnp.dot(normed, wbuf[i], preferred_element_type=F32)
            acc[rows, :] = product if first else acc[rows, :] + product

    def arrived(k):
        project(lax.rem(z + k, NZ))
        project(lax.rem(z - k + NZ, NZ))

    project(z, True)
    arrived(1)
    serve(1)
    arrived(2)
    arrived(3)
    serve(1)
    arrived(4)
    arrived(5)
    serve(1)
    arrived(6)
    serve(1)
    arrived(7)
    serve(2)
    assert served[0] == SUB * NZ // 2
    project(lax.rem(z + NZ // 2, NZ))

    qbuf[z] = acc[:, :HD].astype(BF16)

    def at(way, k, h):
        return (way * FAR + k - 1) * 2 + h

    def piece_at(way, k, j):
        return (way * FAR + k - 1) * SUB + j

    def rows_of(h):
        return pl.ds(pl.multiple_of(h * ROWS, ROWS), ROWS)

    def source(way, k):
        return lax.rem(z + (4 * way - 2) * k + NZ, NZ)

    def along(way):
        return dev(z + 2 - 4 * way, c, x, y)

    def query(way, k, j):
        ref = qbuf.at[source(way, k - 1), pl.ds(pl.multiple_of(j * HB, HB), HB)]
        n = piece_at(way, k, j)
        return remote(ref, ref, q_s.at[n], q_r.at[n], along(way))

    def scores(q, keys):
        s = lax.dot_general(keys, q, (((1,), (1,)), ((), ())), preferred_element_type=F32)
        return s * SCALE

    def part(slot, pairs):
        m = pairs[0][0].max(axis=0, keepdims=True)
        for s, _ in pairs[1:]:
            m = jnp.maximum(m, s.max(axis=0, keepdims=True))
        o = l = None
        for s, vals in pairs:
            p = jnp.exp2(s - m)
            a = jnp.dot(vals[...], p.astype(BF16), preferred_element_type=F32)
            b = p.sum(axis=0, keepdims=True)
            o, l = (a, b) if o is None else (o + a, l + b)
        po[slot] = o
        pt[slot, 0:1] = m
        pt[slot, 1:2] = l

    def old(q):
        return [(scores(q, kold[n]), vold.at[n]) for n in range(2)]

    def new(q, n):
        return scores(q, knew[n]), vnew.at[n]

    def visit(way, k, h):
        slot = at(way, k, h)
        src = source(way, k)

        @pl.when(src > z)
        def _():
            q = qbuf[src, rows_of(h)]
            part(slot, [new(q, 0), new(q, 1)] + old(q))

        @pl.when(src < z)
        def _():
            q = qbuf[src, rows_of(h)]
            part(slot, old(q))

    for j in range(SUB):
        for way in range(2):
            query(way, 1, j).start()
    knew[par] = acc[:, HD : 2 * HD].astype(BF16)
    share(2).start()
    vnew[par] = jnp.transpose(acc[:, 2 * HD :]).astype(BF16)
    share(3).start()

    for cp in csibs:
        cp.wait_send()
    wsib.wait_send()
    hcopy.wait_send()

    @pl.loop(0, SUB * (NZ // 2 - 1))
    def _(n):
        for way in range(2):
            weight(way, n // SUB + 1, lax.rem(n, SUB)).wait_send()

    for j in range(SUB):
        weight(2 * j // SUB, NZ // 2, j).wait_send()
    for copies in one:
        for cp in copies().values():
            cp.wait_send()

    @pl.loop(0, 4)
    def _(o):
        for copies in two:
            for cp in copies(o).values():
                cp.wait_send()

    @pl.loop(0, NX * NY)
    def _(n):
        to_sib(n // NY, lax.rem(n, NY)).wait_send()

    def own(h, earlier):
        q = qbuf[z, rows_of(h)]
        s, vals = new(q, par)
        t = h * ROWS + lax.broadcasted_iota(jnp.int32, s.shape, 1)
        s = jnp.where(lax.broadcasted_iota(jnp.int32, s.shape, 0) <= t, s, -1e30)
        part(4 * FAR + h, [(s, vals)] + earlier(q) + old(q))

    def merged(slot, cols, msg):
        own_m, msg_m = pt[slot, 0:1, cols], tin[msg, 0:1]
        m = jnp.maximum(own_m, msg_m)
        own_f = jnp.exp2(own_m - m)
        msg_f = jnp.exp2(msg_m - m)
        o = po[slot, :, cols] * own_f + oin[msg].astype(F32) * msg_f
        return o, m, pt[slot, 1:2, cols] * own_f + tin[msg, 1:2] * msg_f

    def answer(way, k, j):
        n = piece_at(way, k, j)
        to = along(1 - way)
        return (
            remote(osend.at[n], oin.at[n], o_s.at[n], o_r.at[n], to),
            remote(tsend.at[n], tin.at[n], t_s.at[n], t_r.at[n], to),
        )

    def arrive(way, k, j):
        for cp in answer(way, k + 1, j):
            cp.wait_recv()

    def cols_in(j):
        return pl.ds(pl.multiple_of(lax.rem(j, 2) * HB, HB), HB)

    def give(last, *steps):
        if not last:
            for step in steps:
                arrive(*step)
        for way, k, j in steps:
            slot, cols, n = at(way, k, j // 2), cols_in(j), piece_at(way, k, j)
            if last:
                o, m, l = po[slot, :, cols], pt[slot, 0:1, cols], pt[slot, 1:2, cols]
            else:
                o, m, l = merged(slot, cols, piece_at(way, k + 1, j))
            osend[n] = o.astype(BF16)
            tsend[n, 0:1] = m
            tsend[n, 1:2] = l
        for step in steps:
            for cp in answer(*step):
                cp.start()

    def service(k, h):
        for jj in range(2):
            for way in range(2):
                query(way, k, 2 * h + jj).wait_recv()
                query(way, k + 1, 2 * h + jj).start()

    def visits(k, h):
        @pl.loop(0, 2)
        def _(way):
            visit(way, k, h)

    @pl.loop(0, 2)
    def _(h):
        service(1, h)

    for n in range(4):
        share(n).wait_recv()

    @pl.when(par == 0)
    def _():
        @pl.loop(0, 2)
        def _(h):
            own(h, lambda q: [])

    @pl.when(par == 1)
    def _():
        @pl.loop(0, 2)
        def _(h):
            own(h, lambda q: [new(q, 0)])

    @pl.loop(0, 2)
    def _(h):
        service(2, h)
        visits(1, h)

    @pl.loop(0, 2)
    def _(h):
        for jj in range(2):
            for way in range(2):
                query(way, FAR - 1, 2 * h + jj).wait_recv()
            query(h, FAR, 2 * h + jj).start()
        visits(2, h)

    @pl.loop(0, 2)
    def _(way):
        visit(way, FAR - 1, 1 - way)
        for jj in range(2):
            give(True, (way, FAR - 1, 2 * (1 - way) + jj))

    @pl.loop(0, 2)
    def _(way):
        for jj in range(2):
            query(way, FAR, 2 * way + jj).wait_recv()
        visit(way, FAR, way)
        for jj in range(2):
            give(True, (way, FAR, 2 * way + jj))

    @pl.loop(0, 2)
    def _(way):
        visit(way, FAR - 1, way)

    @pl.loop(0, 8 * FAR - 4)
    def _(n):
        k, way = n // 8 + 1, lax.rem(n, 2)
        j = lax.rem(n // 2, SUB)
        query(way, k, jnp.where(k < FAR, j, 2 * way + j)).wait_send()

    for n in range(4):
        share(n).wait_send()

    @pl.loop(0, 2)
    def _(n):
        give(False, (0, FAR - 1, n), (1, FAR - 1, 2 + n))

    @pl.loop(0, SUB * (FAR - 2))
    def _(n):
        k, p = FAR - 2 - n // SUB, lax.rem(n, SUB)
        give(False, (0, k, lax.rem(p + 2, SUB)), (1, k, p))

    def finish(h):
        slot = 4 * FAR + h
        for jj in range(2):
            cols = pl.ds(jj * HB, HB)
            for way in range(2):
                j = 2 * h + jj
                arrive(way, 0, j)
                o, m, l = merged(slot, cols, piece_at(way, 1, j))
                po[slot, :, cols] = o
                pt[slot, 0:1, cols] = m
                pt[slot, 1:2, cols] = l
        return jnp.transpose(po[slot] / pt[slot, 1:2]).astype(BF16)

    oswap[0] = finish(1 - c)
    swap = remote(oswap.at[0], oswap.at[1], x_s, x_r, sib)
    swap.start()
    out_ref[:, mine] = finish(c)
    swap.wait_recv()
    out_ref[:, theirs] = oswap[1]

    swap.wait_send()

    @pl.loop(0, 8 * FAR - 4)
    def _(n):
        k, way = n // 8 + 1, lax.rem(n, 2)
        j = lax.rem(n // 2, SUB)
        j = jnp.where(k < FAR, j, 2 * way + j)
        for cp in answer(way, k, j):
            cp.wait_send()


def body(hyena_in, prior_kv, filters, gain, w_qkv, cache_k, cache_v):
    hy = jnp.transpose(hyena_in, (1, 0, 2))
    w = jnp.transpose(w_qkv, (1, 0, 2))
    g = gain.reshape(D // HD, HD)
    old = cache_k.shape[0]
    dma = pltpu.SemaphoreType.DMA
    vmem = pltpu.VMEM
    return pl.pallas_call(
        whole_kernel,
        name="whole",
        out_shape=jax.ShapeDtypeStruct((ROWS, WID), BF16),
        in_specs=[pl.BlockSpec(memory_space=pltpu.VMEM)] * 7,
        out_specs=pl.BlockSpec(memory_space=pltpu.VMEM),
        scratch_shapes=[
            vmem((HD, 3 * HD), BF16),
            vmem((NZ, WID, 3 * HD), BF16),
            vmem((ROWS, WID), BF16),
            vmem((TAPS, WID), BF16),
            vmem((TAPS + ROWS + 8, WID), F32),
            vmem((8, TAPS + ROWS, WID), F32),
            vmem((136, WID), F32),
            vmem((2, NX * NY, ROWS, WID), BF16),
            vmem((2 * ROWS, 3 * HD), F32),
            vmem((2 * ROWS, HD), F32),
            dma, dma, dma, dma,
            dma((32,)), dma((32,)), dma((32,)), dma((32,)),
            dma((4,)), dma((4,)), dma((4,)), dma((4,)),
            dma((4, 4)), dma((4, 4)), dma((4, 4)), dma((4, 4)),
            dma((4, 4)), dma((4, 4)),
            vmem((2, old, HD), BF16),
            vmem((2, 2 * old, HD), BF16),
            vmem((2, HD, 2 * old), BF16),
            vmem((2, 2 * ROWS, HD), BF16),
            vmem((2, HD, 2 * ROWS), BF16),
            vmem((NZ, 2 * ROWS, HD), BF16),
            vmem((4 * FAR + 2, HD, ROWS), F32),
            vmem((4 * FAR + 2, 8, ROWS), F32),
            vmem((2 * FAR * SUB, HD, HB), BF16),
            vmem((2 * FAR * SUB, HD, HB), BF16),
            vmem((2 * FAR * SUB, 2, HB), F32),
            vmem((2 * FAR * SUB, 2, HB), F32),
            vmem((2, ROWS, HD), BF16),
            dma((2,)), dma((2,)), dma((4,)), dma((4,)),
            dma((32,)), dma((32,)), dma((32,)), dma((32,)), dma((32,)), dma((32,)),
            dma, dma,
        ],
        compiler_params=pltpu.CompilerParams(
            collective_id=1, has_side_effects=True, vmem_limit_bytes=56 * 1024 * 1024
        ),
    )(hy, prior_kv, filters, g, w, cache_k, cache_v)


def solution(mesh):
    return jax.shard_map(
        body,
        mesh=mesh,
        in_specs=(
            P("seq", None, "chan"),
            P(None, "chan"),
            P("chan", None),
            P(),
            P("seq", None, "chan"),
            P("seq", "chan"),
            P("seq", "chan"),
        ),
        out_specs=P("seq", "chan"),
        check_vma=False,
    )
```

```python
import jax
import jax.numpy as jnp
from jax import lax
from jax.experimental import pallas as pl
from jax.experimental.pallas import tpu as pltpu
from jax.sharding import PartitionSpec as P

MESH = pl.DeviceIdType.MESH
F32 = jnp.float32
BF16 = jnp.bfloat16
NZ = 16
NX = 4
NY = 4
ROWS = 256
WID = 256
HD = 128
TAPS = 128
D = NX * NY * WID
EPS = 1e-6
FAR = 4
SUB = 4
HB = 2 * ROWS // SUB
SCALE = 1.4426950408889634 / HD**0.5


def place():
    s = lax.axis_index("seq")
    i = lax.axis_index("chan")
    return s // 2, lax.rem(s, 2), i // NY, lax.rem(i, NY)


def dev(z, c, x, y):
    return (lax.rem(z + NZ, NZ) * 2 + c, lax.rem(x + NX, NX) * NY + lax.rem(y + NY, NY))


def whole_kernel(
    hy_ref, prior_ref, filt_ref, gain_ref, w_ref, ck_ref, cv_ref, out_ref,
    wsend, wbuf, kvp, halo, ext, shifts, table, hbuf, acc, ssq,
    sib_s, sib_r, halo_s, halo_r, up_s, up_r, dn_s, dn_r,
    a1_s, a1_r, b1_s, b1_r, a2_s, a2_r, b2_s, b2_r, hs_s, hs_r,
    csib, kold, vold, knew, vnew, qbuf, po, pt, osend, oin, tsend, tin, oswap,
    cs_s, cs_r, e_s, e_r, q_s, q_r, o_s, o_r, t_s, t_r, x_s, x_r,
):
    z, c, x, y = place()
    me_i = x * NY + y
    sib = dev(z, 1 - c, x, y)
    above = dev(z + 1, c, x, y)
    below = dev(z - 1, c, x, y)
    nxt = dev(z + c, 1 - c, x, y)
    other = dev(z + 2 * c - 1, 1 - c, x, y)

    def remote(src, dst, ss, rs, to):
        return pltpu.make_async_remote_copy(
            src_ref=src, dst_ref=dst, send_sem=ss, recv_sem=rs, device_id=to, device_id_type=MESH
        )

    barrier = pltpu.get_barrier_semaphore()
    par = lax.rem(z, 2)
    twin = dev(z + 1 - 2 * par, c, x, y)
    partners = [sib, above, below, other, dev(z + 2, c, x, y), dev(z - 2, c, x, y)]
    partners += [dev(z, c, x + d, y) for d in (1, -1)]
    partners += [dev(z, c, x, y + d) for d in (1, -1)]
    for to in partners:
        pl.semaphore_signal(barrier, inc=1, device_id=to, device_id_type=MESH)

    mine = pl.ds(pl.multiple_of(c * HD, HD), HD)
    theirs = pl.ds(pl.multiple_of((1 - c) * HD, HD), HD)
    for j in range(3):
        wbuf[z, mine, j * HD : (j + 1) * HD] = w_ref[j, :, mine]
        wsend[:, j * HD : (j + 1) * HD] = w_ref[j, :, theirs]
    kvp[...] = (hy_ref[1].astype(F32) * hy_ref[2].astype(F32)).astype(BF16)
    pl.semaphore_wait(barrier, len(partners))

    wsib = remote(wsend, wbuf.at[z, mine, :], sib_s, sib_r, sib)
    wsib.start()
    csibs = [
        remote(ref.at[:, theirs], csib.at[n], cs_s.at[n], cs_r.at[n], sib)
        for n, ref in enumerate((ck_ref, cv_ref))
    ]
    for cp in csibs:
        cp.start()
    hcopy = remote(kvp.at[pl.ds(ROWS - TAPS, TAPS)], halo, halo_s, halo_r, nxt)
    hcopy.start()

    def goes(way, k, j):
        return k < NZ // 2 or (k == NZ // 2 and (j < SUB // 2) == (way == 0))

    def weight(way, k, j):
        src = lax.rem(z + (2 * way - 1) * (k - 1) + NZ, NZ)
        row = lax.rem(j + c * (SUB // 2), SUB) * (WID // SUB)
        ref = wbuf.at[src, pl.ds(pl.multiple_of(row, WID // SUB), WID // SUB)]
        n = (k - 1) * SUB + j
        ss, rs = (up_s, up_r) if way == 0 else (dn_s, dn_r)
        return remote(ref, ref, ss.at[n], rs.at[n], (above, below)[way])

    for j in range(SUB // 2):
        for way in range(2):
            weight(way, 1, j).start()

    def ring_next(n):
        k, j = n // SUB + 1, n % SUB
        for way in range(2):
            if goes(way, k, j):
                weight(way, k, j).wait_recv()
            if goes(way, k + 1, j):
                weight(way, k + 1, j).start()

    served = [0]

    def serve(count):
        begin, end = served[0], served[0] + count
        served[0] = end
        looped = min(end, SUB * (NZ // 2 - 2))
        if looped - begin > 1:

            @pl.loop(begin, looped)
            def _(n):
                k, j = n // SUB + 1, lax.rem(n, SUB)
                for way in range(2):
                    weight(way, k, j).wait_recv()
                    weight(way, k + 1, j).start()

            begin = looped
        for n in range(begin, end):
            ring_next(n)

    rev = (
        lax.broadcasted_iota(jnp.int32, (136, TAPS), 0)
        + lax.broadcasted_iota(jnp.int32, (136, TAPS), 1)
        == TAPS
    ).astype(F32)
    groups = filt_ref.shape[0]
    spread = (
        lax.broadcasted_iota(jnp.int32, (groups, WID), 0)
        == lax.broadcasted_iota(jnp.int32, (groups, WID), 1) // (WID // groups)
    ).astype(F32)
    reversed_taps = lax.dot_general(
        rev, filt_ref[...], (((1,), (1,)), ((), ())),
        precision=lax.Precision.HIGHEST, preferred_element_type=F32,
    )
    table[...] = lax.dot_general(
        reversed_taps, spread, (((1,), (0,)), ((), ())),
        precision=lax.Precision.HIGHEST, preferred_element_type=F32,
    )

    wsib.wait_recv()
    for j in range(SUB // 2, SUB):
        for way in range(2):
            weight(way, 1, j).start()
    hcopy.wait_recv()

    ext[pl.ds(0, TAPS), :] = halo[...].astype(F32)

    @pl.when(jnp.logical_and(z == 0, c == 0))
    def _():
        ext[pl.ds(1, TAPS - 1), :] = prior_ref[...].astype(F32)

    ext[pl.ds(TAPS, ROWS), :] = kvp[...].astype(F32)
    ext[pl.ds(TAPS + ROWS, 8), :] = jnp.zeros((8, WID), F32)
    total = TAPS + ROWS
    for r in range(8):
        shifts[r] = ext[r : r + total, :]

    half = ROWS // 2

    def conv_part(rows, lanes):
        def step(a, tot):
            base = pl.multiple_of(a * 8, 8)
            coeffs = table[pl.ds(base, 8), lanes]
            for r in range(8):
                window = shifts[r, pl.ds(pl.multiple_of(base + rows, 8), half), lanes]
                tot = tot + coeffs[r : r + 1] * window
            return tot

        conv = lax.fori_loop(0, TAPS // 8 + 1, step, jnp.zeros((half, HD), F32))
        out = (hy_ref[0, rows : rows + half, lanes].astype(F32) * conv).astype(BF16)
        hbuf[c, me_i, rows : rows + half, lanes] = out

    conv_part(0, slice(0, HD))
    serve(1)
    conv_part(0, slice(HD, WID))
    serve(1)
    conv_part(half, slice(0, HD))
    serve(1)
    conv_part(half, slice(HD, WID))

    quarter = half // 2

    def slot(ex, ey):
        return lax.rem(x - ex + NX, NX) * NY + lax.rem(y - ey + NY, NY)

    def spread_over(block, row, plus, minus, ss, rs):
        def send(e, at, size, to, code):
            ref = hbuf.at[c, block(e), pl.ds(row + at, size)]
            return remote(ref, ref, ss(code), rs(code), to)

        return {
            1: send(0, 0, half, plus, 1),
            3: send(0, 0, half, minus, 3),
            2: send(1, 0, quarter, plus, 2),
            0: send(3, quarter, quarter, minus, 0),
        }

    def at_x(e):
        return slot(e, 0)

    def at_y(e):
        return slot(0, e)

    xs = dev(z, c, x + 1, y), dev(z, c, x - 1, y)
    ys = dev(z, c, x, y + 1), dev(z, c, x, y - 1)
    one = [
        lambda: spread_over(at_x, 0, *xs, lambda n: a1_s.at[n], lambda n: a1_r.at[n]),
        lambda: spread_over(at_y, half, *ys, lambda n: b1_s.at[n], lambda n: b1_r.at[n]),
    ]
    two = [
        lambda o: spread_over(lambda e: slot(o, e), 0, *ys, lambda n: a2_s.at[o, n], lambda n: a2_r.at[o, n]),
        lambda o: spread_over(lambda e: slot(e, o), half, *xs, lambda n: b2_s.at[o, n], lambda n: b2_r.at[o, n]),
    ]

    def start_both(copies):
        copies[1].start()
        copies[3].start()

    def pass_on(copies):
        copies[1].wait_recv()
        copies[2].start()
        copies[3].wait_recv()
        copies[0].start()

    def last_of(copies):
        copies[2].wait_recv()
        copies[0].wait_recv()

    def to_sib(ex, ey):
        ref = hbuf.at[c, slot(ex, ey)]
        return remote(ref, ref, hs_s.at[ex, ey], hs_r.at[ex, ey], sib)

    for copies in one:
        start_both(copies())
    for copies in two:
        start_both(copies(0))
    to_sib(0, 0).start()
    serve(5)
    for n in range(2):
        pass_on(one[n]())
        start_both(two[n](1))
        start_both(two[n](3))
    serve(3)
    for n in range(2):
        last_of(one[n]())
        start_both(two[n](2))
    for n in range(2):
        pass_on(two[n](0))
    serve(3)
    for o in (1, 3):
        for n in range(2):
            pass_on(two[n](o))
        serve(2)
    for key in ((1, 0), (3, 0), (0, 1), (0, 3), (1, 1), (1, 3), (3, 1), (3, 3)):
        to_sib(*key).start()
    for n in range(2):
        last_of(two[n](0))
        pass_on(two[n](2))
    to_sib(2, 0).start()
    to_sib(0, 2).start()
    serve(2)
    for o in (1, 3):
        for n in range(2):
            last_of(two[n](o))
        for key in ((o, 2), (2, o)):
            to_sib(*key).start()
    serve(2)
    for n in range(2):
        last_of(two[n](2))
    to_sib(2, 2).start()
    def share(n):
        ref = (kold, vold, knew, vnew)[n].at[par]
        return remote(ref, ref, e_s.at[n], e_r.at[n], twin)

    for n, ref in enumerate((ck_ref, cv_ref)):
        csibs[n].wait_recv()
        both = jnp.concatenate([ref[:, mine].astype(F32), csib[n].astype(F32)], axis=0)
        if n == 0:
            kold[par] = both.astype(BF16)
        else:
            vold[par] = jnp.transpose(both).astype(BF16)
        share(n).start()
    serve(2)

    ssq[...] = jnp.zeros_like(ssq)

    def squares(h, i):
        blk = hbuf[h, i].astype(F32)
        sq = blk * blk
        ssq[pl.ds(pl.multiple_of(h * ROWS, ROWS), ROWS), :] += sq[:, :HD] + sq[:, HD:]

    @pl.loop(0, NX * NY)
    def _(i):
        squares(c, i)

    @pl.loop(0, NX * NY)
    def _(n):
        ex, ey = n // NY, lax.rem(n, NY)
        to_sib(ex, ey).wait_recv()
        squares(1 - c, slot(ex, ey))

    inv = lax.rsqrt(jnp.sum(ssq[...], axis=1, keepdims=True) * (1.0 / D) + EPS)
    ssq[...] = jnp.broadcast_to(inv, ssq.shape)
    serve(2)

    def project(i, first=False):
        ga, gb = gain_ref[pl.ds(2 * i, 1), :], gain_ref[pl.ds(2 * i + 1, 1), :]
        g = jnp.concatenate([ga, gb], axis=1)
        for h in range(2):
            rows = pl.ds(h * ROWS, ROWS)
            scale = ssq[rows, :]
            scale = jnp.concatenate([scale, scale], axis=1)
            normed = (hbuf[h, i].astype(F32) * scale * g).astype(BF16)
            product = jnp.dot(normed, wbuf[i], preferred_element_type=F32)
            acc[rows, :] = product if first else acc[rows, :] + product

    def arrived(k):
        project(lax.rem(z + k, NZ))
        project(lax.rem(z - k + NZ, NZ))

    project(z, True)
    arrived(1)
    serve(1)
    arrived(2)
    arrived(3)
    serve(1)
    arrived(4)
    arrived(5)
    serve(1)
    arrived(6)
    serve(1)
    arrived(7)
    serve(2)
    assert served[0] == SUB * NZ // 2
    project(lax.rem(z + NZ // 2, NZ))

    qbuf[z] = acc[:, :HD].astype(BF16)

    def at(way, k, h):
        return (way * FAR + k - 1) * 2 + h

    def piece_at(way, k, j):
        return (way * FAR + k - 1) * SUB + j

    def rows_of(h):
        return pl.ds(pl.multiple_of(h * ROWS, ROWS), ROWS)

    def source(way, k):
        return lax.rem(z + (4 * way - 2) * k + NZ, NZ)

    def along(way):
        return dev(z + 2 - 4 * way, c, x, y)

    def query(way, k, j):
        ref = qbuf.at[source(way, k - 1), pl.ds(pl.multiple_of(j * HB, HB), HB)]
        n = piece_at(way, k, j)
        return remote(ref, ref, q_s.at[n], q_r.at[n], along(way))

    def scores(q, keys):
        s = lax.dot_general(keys, q, (((1,), (1,)), ((), ())), preferred_element_type=F32)
        return s * SCALE

    def part(slot, pairs):
        m = pairs[0][0].max(axis=0, keepdims=True)
        for s, _ in pairs[1:]:
            m = jnp.maximum(m, s.max(axis=0, keepdims=True))
        o = l = None
        for s, vals in pairs:
            p = jnp.exp2(s - m)
            a = jnp.dot(vals[...], p.astype(BF16), preferred_element_type=F32)
            b = p.sum(axis=0, keepdims=True)
            o, l = (a, b) if o is None else (o + a, l + b)
        po[slot] = o
        pt[slot, 0:1] = m
        pt[slot, 1:2] = l

    def old(q):
        return [(scores(q, kold[n]), vold.at[n]) for n in range(2)]

    def new(q, n):
        return scores(q, knew[n]), vnew.at[n]

    def visit(way, k, h):
        slot = at(way, k, h)
        src = source(way, k)

        @pl.when(src > z)
        def _():
            q = qbuf[src, rows_of(h)]
            part(slot, [new(q, 0), new(q, 1)] + old(q))

        @pl.when(src < z)
        def _():
            q = qbuf[src, rows_of(h)]
            part(slot, old(q))

    for j in range(SUB):
        for way in range(2):
            query(way, 1, j).start()
    knew[par] = acc[:, HD : 2 * HD].astype(BF16)
    share(2).start()
    vnew[par] = jnp.transpose(acc[:, 2 * HD :]).astype(BF16)
    share(3).start()

    for cp in csibs:
        cp.wait_send()
    wsib.wait_send()
    hcopy.wait_send()

    @pl.loop(0, SUB * (NZ // 2 - 1))
    def _(n):
        for way in range(2):
            weight(way, n // SUB + 1, lax.rem(n, SUB)).wait_send()

    for j in range(SUB):
        weight(2 * j // SUB, NZ // 2, j).wait_send()
    for copies in one:
        for cp in copies().values():
            cp.wait_send()

    @pl.loop(0, 4)
    def _(o):
        for copies in two:
            for cp in copies(o).values():
                cp.wait_send()

    @pl.loop(0, NX * NY)
    def _(n):
        to_sib(n // NY, lax.rem(n, NY)).wait_send()

    def own(h, earlier):
        q = qbuf[z, rows_of(h)]
        s, vals = new(q, par)
        t = h * ROWS + lax.broadcasted_iota(jnp.int32, s.shape, 1)
        s = jnp.where(lax.broadcasted_iota(jnp.int32, s.shape, 0) <= t, s, -1e30)
        part(4 * FAR + h, [(s, vals)] + earlier(q) + old(q))

    def merged(slot, cols, msg):
        own_m, msg_m = pt[slot, 0:1, cols], tin[msg, 0:1]
        m = jnp.maximum(own_m, msg_m)
        own_f = jnp.exp2(own_m - m)
        msg_f = jnp.exp2(msg_m - m)
        o = po[slot, :, cols] * own_f + oin[msg].astype(F32) * msg_f
        return o, m, pt[slot, 1:2, cols] * own_f + tin[msg, 1:2] * msg_f

    def answer(way, k, j):
        n = piece_at(way, k, j)
        to = along(1 - way)
        return (
            remote(osend.at[n], oin.at[n], o_s.at[n], o_r.at[n], to),
            remote(tsend.at[n], tin.at[n], t_s.at[n], t_r.at[n], to),
        )

    def arrive(way, k, j):
        for cp in answer(way, k + 1, j):
            cp.wait_recv()

    def cols_in(j):
        return pl.ds(pl.multiple_of(lax.rem(j, 2) * HB, HB), HB)

    def give(last, *steps):
        if not last:
            for step in steps:
                arrive(*step)
        for way, k, j in steps:
            slot, cols, n = at(way, k, j // 2), cols_in(j), piece_at(way, k, j)
            if last:
                o, m, l = po[slot, :, cols], pt[slot, 0:1, cols], pt[slot, 1:2, cols]
            else:
                o, m, l = merged(slot, cols, piece_at(way, k + 1, j))
            osend[n] = o.astype(BF16)
            tsend[n, 0:1] = m
            tsend[n, 1:2] = l
        for step in steps:
            for cp in answer(*step):
                cp.start()

    def service(k, h):
        for jj in range(2):
            for way in range(2):
                query(way, k, 2 * h + jj).wait_recv()
                query(way, k + 1, 2 * h + jj).start()

    def visits(k, h):
        @pl.loop(0, 2)
        def _(way):
            visit(way, k, h)

    @pl.loop(0, 2)
    def _(h):
        service(1, h)

    for n in range(2):
        share(n).wait_recv()

    @pl.when(par == 0)
    def _():
        @pl.loop(0, 2)
        def _(h):
            own(h, lambda q: [])

    for n in range(2, 4):
        share(n).wait_recv()

    @pl.when(par == 1)
    def _():
        @pl.loop(0, 2)
        def _(h):
            own(h, lambda q: [new(q, 0)])

    @pl.loop(0, 2)
    def _(h):
        service(2, h)
        visits(1, h)

    @pl.loop(0, 2)
    def _(h):
        for jj in range(2):
            for way in range(2):
                query(way, FAR - 1, 2 * h + jj).wait_recv()
            query(h, FAR, 2 * h + jj).start()
        visits(2, h)

    @pl.loop(0, 2)
    def _(way):
        visit(way, FAR - 1, 1 - way)
        for jj in range(2):
            give(True, (way, FAR - 1, 2 * (1 - way) + jj))

    @pl.loop(0, 2)
    def _(way):
        for jj in range(2):
            query(way, FAR, 2 * way + jj).wait_recv()
        visit(way, FAR, way)
        for jj in range(2):
            give(True, (way, FAR, 2 * way + jj))

    @pl.loop(0, 2)
    def _(way):
        visit(way, FAR - 1, way)

    @pl.loop(0, 8 * FAR - 4)
    def _(n):
        k, way = n // 8 + 1, lax.rem(n, 2)
        j = lax.rem(n // 2, SUB)
        query(way, k, jnp.where(k < FAR, j, 2 * way + j)).wait_send()

    for n in range(4):
        share(n).wait_send()

    @pl.loop(0, 2)
    def _(n):
        give(False, (0, FAR - 1, n), (1, FAR - 1, 2 + n))

    @pl.loop(0, SUB * (FAR - 2))
    def _(n):
        k, p = FAR - 2 - n // SUB, lax.rem(n, SUB)
        give(False, (0, k, lax.rem(p + 2, SUB)), (1, k, p))

    def finish(h):
        slot = 4 * FAR + h
        for jj in range(2):
            cols = pl.ds(jj * HB, HB)
            for way in range(2):
                j = 2 * h + jj
                arrive(way, 0, j)
                o, m, l = merged(slot, cols, piece_at(way, 1, j))
                po[slot, :, cols] = o
                pt[slot, 0:1, cols] = m
                pt[slot, 1:2, cols] = l
        return jnp.transpose(po[slot] / pt[slot, 1:2]).astype(BF16)

    oswap[0] = finish(1 - c)
    swap = remote(oswap.at[0], oswap.at[1], x_s, x_r, sib)
    swap.start()
    out_ref[:, mine] = finish(c)
    swap.wait_recv()
    out_ref[:, theirs] = oswap[1]

    swap.wait_send()

    @pl.loop(0, 8 * FAR - 4)
    def _(n):
        k, way = n // 8 + 1, lax.rem(n, 2)
        j = lax.rem(n // 2, SUB)
        j = jnp.where(k < FAR, j, 2 * way + j)
        for cp in answer(way, k, j):
            cp.wait_send()


def body(hyena_in, prior_kv, filters, gain, w_qkv, cache_k, cache_v):
    hy = jnp.transpose(hyena_in, (1, 0, 2))
    w = jnp.transpose(w_qkv, (1, 0, 2))
    g = gain.reshape(D // HD, HD)
    old = cache_k.shape[0]
    dma = pltpu.SemaphoreType.DMA
    vmem = pltpu.VMEM
    return pl.pallas_call(
        whole_kernel,
        name="whole",
        out_shape=jax.ShapeDtypeStruct((ROWS, WID), BF16),
        in_specs=[pl.BlockSpec(memory_space=pltpu.VMEM)] * 7,
        out_specs=pl.BlockSpec(memory_space=pltpu.VMEM),
        scratch_shapes=[
            vmem((HD, 3 * HD), BF16),
            vmem((NZ, WID, 3 * HD), BF16),
            vmem((ROWS, WID), BF16),
            vmem((TAPS, WID), BF16),
            vmem((TAPS + ROWS + 8, WID), F32),
            vmem((8, TAPS + ROWS, WID), F32),
            vmem((136, WID), F32),
            vmem((2, NX * NY, ROWS, WID), BF16),
            vmem((2 * ROWS, 3 * HD), F32),
            vmem((2 * ROWS, HD), F32),
            dma, dma, dma, dma,
            dma((32,)), dma((32,)), dma((32,)), dma((32,)),
            dma((4,)), dma((4,)), dma((4,)), dma((4,)),
            dma((4, 4)), dma((4, 4)), dma((4, 4)), dma((4, 4)),
            dma((4, 4)), dma((4, 4)),
            vmem((2, old, HD), BF16),
            vmem((2, 2 * old, HD), BF16),
            vmem((2, HD, 2 * old), BF16),
            vmem((2, 2 * ROWS, HD), BF16),
            vmem((2, HD, 2 * ROWS), BF16),
            vmem((NZ, 2 * ROWS, HD), BF16),
            vmem((4 * FAR + 2, HD, ROWS), F32),
            vmem((4 * FAR + 2, 8, ROWS), F32),
            vmem((2 * FAR * SUB, HD, HB), BF16),
            vmem((2 * FAR * SUB, HD, HB), BF16),
            vmem((2 * FAR * SUB, 2, HB), F32),
            vmem((2 * FAR * SUB, 2, HB), F32),
            vmem((2, ROWS, HD), BF16),
            dma((2,)), dma((2,)), dma((4,)), dma((4,)),
            dma((32,)), dma((32,)), dma((32,)), dma((32,)), dma((32,)), dma((32,)),
            dma, dma,
        ],
        compiler_params=pltpu.CompilerParams(
            collective_id=1, has_side_effects=True, vmem_limit_bytes=56 * 1024 * 1024
        ),
    )(hy, prior_kv, filters, g, w, cache_k, cache_v)


def solution(mesh):
    return jax.shard_map(
        body,
        mesh=mesh,
        in_specs=(
            P("seq", None, "chan"),
            P(None, "chan"),
            P("chan", None),
            P(),
            P("seq", None, "chan"),
            P("seq", "chan"),
            P("seq", "chan"),
        ),
        out_specs=P("seq", "chan"),
        check_vma=False,
    )
```
